32 devices in a mesh: fsdp: 8 (over z, core), seq: 4 (over y, x).
Axes of the slice: x: 2, y: 2, z: 4, core: 2. Of those that a mesh axis runs over, the one named last changes fastest.
Arguments:
- tokens: bfloat16 [16384, 2048], P(('fsdp', 'seq')), may hold values from -6 to 6
- mixed_cotangent: bfloat16 [16384, 2048], P(('fsdp', 'seq')), may hold values from -6 to 6
- lengths: int32 [8, 3], P('fsdp'), may hold values from 1 to 1024, 2048 in all within a row
- owner_slot: int32 [16384], P(('fsdp', 'seq')), may hold values from 0 to 16383, as said below
- q_weight: bfloat16 [2048, 2048], P('fsdp'), may hold values from -0.125 to 0.125
- key_projection: bfloat16 [2048, 512], P('fsdp'), may hold values from -0.125 to 0.125
- value_projection: bfloat16 [2048, 512], P('fsdp'), may hold values from -0.125 to 0.125
- out_weight: bfloat16 [2048, 2048], P('fsdp'), may hold values from -1 to 1
- gate_weight: bfloat16 [2048, 8192], P('fsdp'), may hold values from -0.125 to 0.125
- up_weight: bfloat16 [2048, 8192], P('fsdp'), may hold values from -0.125 to 0.125
- down_weight: bfloat16 [2048, 8192], P('fsdp'), may hold values from -0.0625 to 0.0625
- attn_gain: bfloat16 [2048], P('fsdp'), may hold values from 0.25 to 1.75
- ffn_gain: bfloat16 [2048], P('fsdp'), may hold values from 0.25 to 1.75
- query_gain: bfloat16 [64], replicated, may hold values from 0.25 to 1.75
- key_gain: bfloat16 [64], replicated, may hold values from 0.25 to 1.75
Outputs:
- mixed: bfloat16 [16384, 2048], P(('fsdp', 'seq'))
- input_grad: bfloat16 [16384, 2048], P(('fsdp', 'seq'))
- q_weight_grad: float32 [2048, 2048], P('fsdp')
- k_weight_grad: float32 [2048, 512], P('fsdp')
- v_weight_grad: float32 [2048, 512], P('fsdp')
- out_weight_grad: float32 [2048, 2048], P('fsdp')
- gate_weight_grad: float32 [2048, 8192], P('fsdp')
- up_weight_grad: float32 [2048, 8192], P('fsdp')
- down_weight_grad: float32 [2048, 8192], P('fsdp')
- attn_gain_grad: float32 [2048], P('fsdp')
- ffn_gain_grad: float32 [2048], P('fsdp')
- query_gain_grad: float32 [64], replicated
- key_gain_grad: float32 [64], replicated
The draws below stay inside these ranges and needn't reach their ends.
Inputs may be any that keep to these rules, and one draw needn't show every extreme that they name: owner_slot is a permutation of the token positions. Write a given position p as (f * 4 + s) * 512 + r with r < 512, s < 4; its owner position q is (j * 4 + s) * 512 + f * 64 + t for some j < 8 and t < 64: a token keeps its index s along seq, and each device gives exactly 64 tokens to each owner in its column. lengths[g] lists the sequences of owned group g in order and sums to 2048.
All inputs are finite; a program needn't handle non-finite values.
Results may differ from the reference program's by a relative error of at most 0.022.
Values may be sent and summed in bfloat16 or wider, within the bound.
A program may use at most 512 MiB of HBM per device.

```python
import math
import jax
import jax.numpy as jnp
import numpy as np
from jax import lax

D = 2048
FF = 8192
QUERY_HEADS = 32
KEY_VALUE_HEADS = 8
HEAD_SIZE = 64
QW = 2048
KW = 512
SEQS_G = 3
GROUP_TOKENS = 2048
TOK_DEV = 512
TOKENS = 16384
GROUPS = 8
RANKS = 4
SLICE = 64
LONGEST = 1024
QUERY_BLOCK_ROWS = 512


def draw_owner_slot(key, part):
    device_keys = jax.random.split(jax.random.fold_in(key, 11), GROUPS * RANKS)
    slot_table = jax.vmap(lambda device_key: jax.random.permutation(device_key, TOK_DEV))(device_keys).astype(jnp.int32)
    device_ids = jnp.arange(GROUPS * RANKS, dtype=jnp.int32)
    group_ids = (device_ids // RANKS)[:, None]
    rank_ids = (device_ids % RANKS)[:, None]
    target = slot_table // SLICE
    owner = (target * RANKS + rank_ids) * TOK_DEV + group_ids * SLICE + slot_table % SLICE
    return owner.reshape(-1).astype(jnp.int32)


def level_of(stream_key, dims, pieces, least, largest):
    def one(axis_at, shards_of):
        heights = jax.random.uniform(jax.random.fold_in(jax.random.fold_in(stream_key, 6), axis_at), (shards_of,), jnp.float32, least / len(pieces), largest / len(pieces))
        return jnp.repeat(jnp.exp(heights), dims[axis_at] // shards_of).reshape((-1,) + (1,) * (len(dims) - axis_at - 1))

    factor_of = one(*pieces[0])
    for cut in pieces[1:]:
        factor_of = factor_of * one(*cut)
    return factor_of


def profile(amount, total, bound, lean):
    weights = [(1 << 20) // math.isqrt(grade ** lean) + 1 for grade in range(2, amount + 1)]
    surplus, given = total - bound - (amount - 1), [1] * (amount - 1)
    while surplus > 0:
        candidates = [i for i in range(amount - 1) if given[i] < bound]
        whole, budget = sum([weights[i] for i in candidates]), surplus
        for i in candidates:
            addition = min(bound - given[i], max(1, budget * weights[i] // whole), surplus)
            given[i] = given[i] + addition
            surplus = surplus - addition
    return np.array([bound] + given)


def ragged(own_key, amount, total, most, skew):
    if amount == 2:
        one = jax.random.randint(own_key, (), max(1, total - most), min(most, total - 1) + 1)
        return jnp.stack([one, total - one])
    sizes = jnp.asarray(profile(amount, total, most, skew), jnp.int32)
    twos = (amount - 1) // 2
    donor, sink = sizes[1:1 + 2 * twos:2], sizes[2:2 + 2 * twos:2]
    margin = jnp.minimum(donor - 1, most - sink)
    shifted = jax.random.randint(jax.random.fold_in(own_key, 1), (twos,), 0, 1 << 20) % (margin + 1)
    sizes = sizes.at[1:1 + 2 * twos:2].set(donor - shifted).at[2:2 + 2 * twos:2].set(sink + shifted)
    return sizes[jax.random.permutation(jax.random.fold_in(own_key, 2), amount)]


def centred(rng, dims, scale, bound, pieces=(), kind=jnp.bfloat16):
    level = level_of(rng, dims, pieces, -0.22, 0.18) if pieces else 1.0
    drawn = jax.random.normal(rng, dims, jnp.float32) * scale * level
    return jnp.minimum(jnp.maximum(drawn, -bound), bound).astype(kind)


def setup_inputs(seed: int = 0) -> dict:
    splits = jax.random.split(jax.random.key(seed), 16)
    return {
        "tokens": centred(splits[0], (TOKENS, D), 1.0, 6.0, ((0, 32),)),
        "mixed_cotangent": centred(splits[1], (TOKENS, D), 1.0, 6.0, ((0, 32),)),
        "lengths": jax.vmap(lambda own: ragged(own, SEQS_G, GROUP_TOKENS, LONGEST, 2))(jax.random.split(splits[2], GROUPS)).reshape((GROUPS, SEQS_G)).astype(jnp.int32),
        "owner_slot": draw_owner_slot(jax.random.fold_in(splits[15], 71), 0),
        "q_weight": centred(splits[4], (D, QW), D ** -0.5, 0.125, ((0, 8),)),
        "key_projection": centred(splits[5], (D, KW), D ** -0.5, 0.125, ((0, 8),)),
        "value_projection": centred(splits[6], (D, KW), D ** -0.5, 0.125, ((0, 8),)),
        "out_weight": centred(splits[7], (D, QW), (QW // 64) ** -0.5, 1.0, ((0, 8),)),
        "gate_weight": centred(splits[8], (D, FF), D ** -0.5, 0.125, ((0, 8),)),
        "up_weight": centred(splits[9], (D, FF), D ** -0.5, 0.125, ((0, 8),)),
        "down_weight": centred(splits[10], (D, FF), FF ** -0.5, 0.0625, ((0, 8),)),
        "attn_gain": jnp.clip(1.0 + 0.15 * jax.random.normal(splits[11], (D,), jnp.float32), 0.25, 1.75).astype(jnp.bfloat16),
        "ffn_gain": jnp.clip(1.0 + 0.15 * jax.random.normal(splits[12], (D,), jnp.float32), 0.25, 1.75).astype(jnp.bfloat16),
        "query_gain": jnp.clip(1.0 + 0.15 * jax.random.normal(splits[13], (HEAD_SIZE,), jnp.float32), 0.25, 1.75).astype(jnp.bfloat16),
        "key_gain": jnp.clip(1.0 + 0.15 * jax.random.normal(splits[14], (HEAD_SIZE,), jnp.float32), 0.25, 1.75).astype(jnp.bfloat16),
    }


EPS = 1e-05
THETA = 1000000.0
NEGATIVE = -1e+30

@jax.custom_vjp
def lower_precision(v):
    return lax.optimization_barrier(v.astype(jnp.bfloat16)).astype(jnp.float32)

@jax.custom_vjp
def lower_precision_backward(v):
    return v

def low_keep(v):
    return (lower_precision(v), None)

def low_pass(kept, grad):
    return (grad,)

def back_keep(v):
    return (v, None)

def back_low(kept, grad):
    return (lower_precision(grad),)
lower_precision.defvjp(low_keep, low_pass)
lower_precision_backward.defvjp(back_keep, back_low)

def rms_normalize(values, gain_vector):
    return values * lax.rsqrt(lax.optimization_barrier(jnp.mean(values * values, axis=-1, keepdims=True)) + EPS) * gain_vector

def rotary_apply(values, cosine_table, sine_table):
    middle = values.shape[-1] // 2
    first_half = values[..., :middle]
    second_half = values[..., middle:]
    return jnp.concatenate([first_half * cosine_table - second_half * sine_table, second_half * cosine_table + first_half * sine_table], axis=-1)

def layout(lengths_row, offset, number):
    token_spots = offset + jnp.arange(number, dtype=jnp.int32)
    seq_ends = jnp.cumsum(lengths_row).astype(jnp.int32)
    passed = token_spots[:, None] >= seq_ends[None, :]
    document_index = lax.optimization_barrier(jnp.sum(passed.astype(jnp.int32), axis=1)).astype(jnp.int32)
    starts = lax.optimization_barrier(jnp.sum(jnp.where(passed, lengths_row[None, :], 0), axis=1)).astype(jnp.int32)
    places = (token_spots - starts).astype(jnp.float32)
    freqs = jnp.exp(jnp.arange(HEAD_SIZE // 2, dtype=jnp.float32) * (-2.0 * math.log(THETA) / HEAD_SIZE))
    angles = places[:, None] * freqs[None, :]
    return (document_index, jnp.cos(angles)[:, None, :], jnp.sin(angles)[:, None, :])

def attend_heads(query_head_rows, key_head_rows, value_head_rows, document_index):
    count_blocks = GROUP_TOKENS // QUERY_BLOCK_ROWS
    highest_precision = lax.Precision.HIGHEST
    query_block_list = query_head_rows.reshape(count_blocks, QUERY_BLOCK_ROWS, KEY_VALUE_HEADS, QUERY_HEADS // KEY_VALUE_HEADS, HEAD_SIZE)
    row_table = jnp.arange(GROUP_TOKENS, dtype=jnp.int32).reshape(count_blocks, QUERY_BLOCK_ROWS)
    doc_blocks = document_index.reshape(count_blocks, QUERY_BLOCK_ROWS)
    key_spots = jnp.arange(GROUP_TOKENS, dtype=jnp.int32)

    def block_fn(block_item):
        query_block, row_ids, row_docs = block_item
        scores = jnp.einsum('qhgd,khd->hgqk', query_block, key_head_rows, precision=highest_precision)
        scores = lower_precision_backward(scores * (1.0 / math.sqrt(HEAD_SIZE)))
        allowed = (row_docs[:, None] == document_index[None, :]) & (key_spots[None, :] <= row_ids[:, None])
        scores = jnp.where(allowed[None, None], scores, NEGATIVE)
        row_max = lax.optimization_barrier(jnp.max(scores, axis=-1, keepdims=True))
        exp_scores = jnp.exp(scores - row_max)
        weights = lower_precision(exp_scores / lax.optimization_barrier(jnp.sum(exp_scores, axis=-1, keepdims=True)))
        return jnp.einsum('hgqk,khd->qhgd', weights, value_head_rows, precision=highest_precision)
    output_rows = lax.map(jax.checkpoint(block_fn), (query_block_list, row_table, doc_blocks))
    return output_rows.reshape(GROUP_TOKENS, KEY_VALUE_HEADS, QUERY_HEADS // KEY_VALUE_HEADS, HEAD_SIZE)

def group_block(param_set, tok_group, lengths_row):
    q_weight, key_projection, value_projection, out_weight, gate_weight, up_weight, down_weight, attn_gain, ffn_gain, query_gain, key_gain = param_set
    highest_precision = lax.Precision.HIGHEST
    document_index, cosine_table, sine_table = layout(lengths_row, 0, GROUP_TOKENS)
    normalized_rows = lower_precision(rms_normalize(tok_group, attn_gain))
    query_raw = lower_precision_backward(jnp.dot(normalized_rows, q_weight, precision=highest_precision)).reshape(GROUP_TOKENS, QUERY_HEADS, HEAD_SIZE)
    key_unrotated = lower_precision_backward(jnp.dot(normalized_rows, key_projection, precision=highest_precision)).reshape(GROUP_TOKENS, KEY_VALUE_HEADS, HEAD_SIZE)
    value_head_rows = lower_precision(lower_precision_backward(jnp.dot(normalized_rows, value_projection, precision=highest_precision))).reshape(GROUP_TOKENS, KEY_VALUE_HEADS, HEAD_SIZE)
    query_head_rows = lower_precision(lower_precision_backward(rotary_apply(rms_normalize(query_raw, query_gain), cosine_table, sine_table)))
    key_head_rows = lower_precision(lower_precision_backward(rotary_apply(rms_normalize(key_unrotated, key_gain), cosine_table, sine_table)))
    attention_output = attend_heads(query_head_rows.reshape(GROUP_TOKENS, KEY_VALUE_HEADS, QUERY_HEADS // KEY_VALUE_HEADS, HEAD_SIZE), key_head_rows, value_head_rows, document_index)
    attention_output = lower_precision(lower_precision_backward(attention_output)).reshape(GROUP_TOKENS, QUERY_HEADS * HEAD_SIZE)
    branch = lower_precision_backward(jnp.dot(attention_output, out_weight.T, precision=highest_precision))
    resid = tok_group + branch
    normed_two = lower_precision(rms_normalize(resid, ffn_gain))
    gate_pre = lower_precision_backward(jnp.dot(normed_two, gate_weight, precision=highest_precision))
    up_pre = lower_precision_backward(jnp.dot(normed_two, up_weight, precision=highest_precision))
    hidden = lower_precision(gate_pre * jax.nn.sigmoid(gate_pre) * up_pre)
    return resid + jnp.dot(hidden, down_weight.T, precision=highest_precision)

def reference(tokens, mixed_cotangent, lengths, owner_slot, q_weight, key_projection, value_projection, out_weight, gate_weight, up_weight, down_weight, attn_gain, ffn_gain, query_gain, key_gain):
    inverse = jnp.zeros((TOKENS,), jnp.int32).at[owner_slot].set(jnp.arange(TOKENS, dtype=jnp.int32))
    owned = tokens.astype(jnp.float32)[inverse].reshape(GROUPS, GROUP_TOKENS, D)
    cot_owned = mixed_cotangent.astype(jnp.float32)[inverse].reshape(GROUPS, GROUP_TOKENS, D)
    param_set = (q_weight.astype(jnp.float32), key_projection.astype(jnp.float32), value_projection.astype(jnp.float32), out_weight.astype(jnp.float32), gate_weight.astype(jnp.float32), up_weight.astype(jnp.float32), down_weight.astype(jnp.float32), attn_gain.astype(jnp.float32), ffn_gain.astype(jnp.float32), query_gain.astype(jnp.float32), key_gain.astype(jnp.float32))

    def forward(params_in, owned_tokens):

        def scan_step(carry_state, pair_item):
            return (carry_state, jax.checkpoint(group_block)(params_in, pair_item[0], pair_item[1]))
        _, output_rows = lax.scan(scan_step, jnp.zeros((), jnp.float32), (owned_tokens, lengths))
        return output_rows
    output_rows, pullback = jax.vjp(forward, param_set, owned)
    param_grads, token_grads = pullback(cot_owned)
    mixed = output_rows.reshape(TOKENS, D)[owner_slot].astype(jnp.bfloat16)
    input_grad = token_grads.reshape(TOKENS, D)[owner_slot].astype(jnp.bfloat16)
    return (mixed, input_grad, param_grads[0], param_grads[1], param_grads[2], param_grads[3], param_grads[4], param_grads[5], param_grads[6], param_grads[7], param_grads[8], param_grads[9], param_grads[10])
```

```python
import functools
import math

import jax
import jax.numpy as jnp
from jax import lax
from jax.experimental import pallas as pl
from jax.experimental.pallas import tpu as pltpu
from jax.sharding import PartitionSpec as P

QUERY_HEADS = 32
KEY_VALUE_HEADS = 8
HEAD_SIZE = 64
HALF = HEAD_SIZE // 2
GROUP_HEADS = QUERY_HEADS // KEY_VALUE_HEADS

EPS = 1e-05
THETA = 1000000.0
SCALE = 1.0 / math.sqrt(HEAD_SIZE)
LOG2E = math.log2(math.e)
F32 = jnp.float32
BF16 = jnp.bfloat16


def dot(left, right, left_dim, right_dim):
    return lax.dot_general(
        left, right, (((left_dim,), (right_dim,)), ((), ())), preferred_element_type=F32
    )


def rms_rope(raw, gain, cosine, sine):
    normed = raw * lax.rsqrt(jnp.mean(raw * raw, axis=0, keepdims=True) + EPS) * gain
    first, second = normed[:HALF], normed[HALF:]
    return jnp.concatenate(
        [first * cosine - second * sine, second * cosine + first * sine], axis=0
    )


def rms_rope_back(raw, gain, cosine, sine, grad):
    first, second = grad[:HALF], grad[HALF:]
    turned = jnp.concatenate(
        [first * cosine + second * sine, second * cosine - first * sine], axis=0
    )
    scale = lax.rsqrt(jnp.mean(raw * raw, axis=0, keepdims=True) + EPS)
    unit = raw * scale
    weighted = gain * turned
    raw_grad = scale * (weighted - unit * jnp.mean(weighted * unit, axis=0, keepdims=True))
    return raw_grad, turned * unit


def attend_kernel(
    block, low_ref, order_ref, q_raw, k_raw, v_raw, start_ref, cos_ref, sin_ref, gains_ref,
    out_ref, q_out, k_out, v_out, lse_ref, k_rows, acc, total,
):
    step = pl.program_id(1)
    query_gain, key_gain = gains_ref[0], gains_ref[1]

    @pl.when(step == 0)
    def _():
        token_rows = k_raw.shape[2]
        for r in range(k_raw.shape[0]):
            part = slice(r * token_rows, (r + 1) * token_rows)
            at = order_ref[r]
            key = rms_rope(k_raw[at], key_gain, cos_ref[:, part], sin_ref[:, part])
            k_out[:, part] = key.astype(BF16)
            k_rows[part, :] = key.T.astype(BF16)
            v_out[:, part] = v_raw[at].astype(BF16)

    columns = pl.ds(pl.multiple_of(step * block, block), block)
    cosine, sine = cos_ref[:, columns], sin_ref[:, columns]
    for g in range(GROUP_HEADS):
        rows = slice(g * HEAD_SIZE, (g + 1) * HEAD_SIZE)
        q_out[rows, :] = rms_rope(q_raw[0, rows, :], query_gain, cosine, sine).astype(BF16)
    acc[...] = jnp.zeros_like(acc)
    total[...] = jnp.zeros_like(total)
    starts = start_ref[...]
    spots = step * block + lax.broadcasted_iota(jnp.int32, (1, block), 1)

    def inner(j, carry):
        keys = pl.ds(pl.multiple_of(j * block, block), block)
        key_rows = k_rows[keys, :]
        value = v_out[:, keys]
        key_spots = j * block + lax.broadcasted_iota(jnp.int32, (block, 1), 0)
        allowed = (key_spots >= starts) & (key_spots <= spots)
        for g in range(GROUP_HEADS):
            rows = slice(g * HEAD_SIZE, (g + 1) * HEAD_SIZE)
            score = dot(key_rows, q_out[rows, :], 1, 0)
            prob = jnp.where(allowed, jnp.exp2(score * (SCALE * LOG2E)), 0.0)
            total[g : g + 1, :] += jnp.sum(prob, axis=0, keepdims=True)
            acc[rows, :] += dot(value, prob.astype(BF16), 1, 0)
        return carry

    lax.fori_loop(low_ref[step], step + 1, inner, 0)
    for g in range(GROUP_HEADS):
        rows = slice(g * HEAD_SIZE, (g + 1) * HEAD_SIZE)
        summed = total[g : g + 1, :]
        out_ref[0, rows, :] = (acc[rows, :] / summed).astype(BF16)
        lse_ref[0, g : g + 1, :] = jnp.log2(summed)


def attend_back_kernel(
    block, spans, low_ref, order_ref, q_raw, k_raw, start_ref, cos_ref, sin_ref, gains_ref,
    q_ref, k_ref, v_ref, lse_ref, out_ref, grad_ref,
    d_ref, gain_out, k_rows, v_rows, dq, dk, dv, gain_acc,
):
    head, step = pl.program_id(0), pl.program_id(1)
    steps = pl.num_programs(1)
    local = pl.num_programs(0)
    query_gain, key_gain = gains_ref[0], gains_ref[1]
    width = GROUP_HEADS * HEAD_SIZE
    token_rows = spans * block

    @pl.when((head == 0) & (step == 0))
    def _():
        gain_acc[...] = jnp.zeros_like(gain_acc)
        gain_out[...] = jnp.zeros_like(gain_out)

    @pl.when(step == 0)
    def _():
        k_rows[...] = k_ref[...].astype(F32).T.astype(BF16)
        v_rows[...] = v_ref[...].astype(F32).T.astype(BF16)
        dk[...] = jnp.zeros_like(dk)
        dv[...] = jnp.zeros_like(dv)

    columns = pl.ds(pl.multiple_of(step * block, block), block)
    cosine, sine = cos_ref[:, columns], sin_ref[:, columns]
    dq[...] = jnp.zeros_like(dq)
    starts = start_ref[...]
    spots = step * block + lax.broadcasted_iota(jnp.int32, (1, block), 1)
    inner_sums = [
        jnp.sum(
            out_ref[0, g * HEAD_SIZE : (g + 1) * HEAD_SIZE, :].astype(F32)
            * grad_ref[0, g * HEAD_SIZE : (g + 1) * HEAD_SIZE, :].astype(F32),
            axis=0,
            keepdims=True,
        )
        for g in range(GROUP_HEADS)
    ]

    def inner(j, carry):
        keys = pl.ds(pl.multiple_of(j * block, block), block)
        key_rows, value_rows, key = k_rows[keys, :], v_rows[keys, :], k_ref[:, keys]
        key_spots = j * block + lax.broadcasted_iota(jnp.int32, (block, 1), 0)
        allowed = (key_spots >= starts) & (key_spots <= spots)
        key_sum = jnp.zeros((HEAD_SIZE, block), F32)
        value_sum = jnp.zeros((HEAD_SIZE, block), F32)
        for g in range(GROUP_HEADS):
            rows = slice(g * HEAD_SIZE, (g + 1) * HEAD_SIZE)
            query, grad = q_ref[rows, :], grad_ref[0, rows, :]
            score = dot(key_rows, query, 1, 0) * (SCALE * LOG2E) - lse_ref[0, g : g + 1, :]
            prob = jnp.where(allowed, jnp.exp2(score), 0.0)
            prob_grad = dot(value_rows, grad, 1, 0)
            score_grad = (prob * (prob_grad - inner_sums[g])).astype(BF16)
            value_sum += dot(grad, prob.astype(BF16), 1, 1)
            key_sum += dot(query, score_grad, 1, 1)
            dq[rows, :] += dot(key, score_grad, 1, 0)
        dk[:, keys] += key_sum
        dv[:, keys] += value_sum
        return carry

    lax.fori_loop(low_ref[step], step + 1, inner, 0)
    span = step // spans
    inside = pl.ds(pl.multiple_of((step % spans) * block, block), block)
    for g in range(GROUP_HEADS):
        rows = slice(g * HEAD_SIZE, (g + 1) * HEAD_SIZE)
        grad = (dq[rows, :] * SCALE).astype(BF16).astype(F32)
        raw_grad, terms = rms_rope_back(q_raw[0, rows, :], query_gain, cosine, sine, grad)
        d_ref[order_ref[span], pl.ds(pl.multiple_of(head * width + g * HEAD_SIZE, HEAD_SIZE), HEAD_SIZE), inside] = (
            raw_grad.astype(BF16)
        )
        gain_acc[...] += terms

    @pl.when(step == steps - 1)
    def _():
        key_at = pl.ds(pl.multiple_of(local * width + head * HEAD_SIZE, HEAD_SIZE), HEAD_SIZE)
        value_at = pl.ds(
            pl.multiple_of(local * (width + HEAD_SIZE) + head * HEAD_SIZE, HEAD_SIZE), HEAD_SIZE
        )
        for r in range(d_ref.shape[0]):
            part = slice(r * token_rows, (r + 1) * token_rows)
            grad = (dk[:, part] * SCALE).astype(BF16).astype(F32)
            raw_grad, terms = rms_rope_back(
                k_raw[order_ref[r]], key_gain, cos_ref[:, part], sin_ref[:, part], grad
            )
            d_ref[order_ref[r], key_at, :] = raw_grad.astype(BF16)
            d_ref[order_ref[r], value_at, :] = dv[:, part].astype(BF16)
            gain_out[1] += jnp.broadcast_to(
                jnp.sum(terms, axis=1, keepdims=True), gain_out.shape[1:]
            )

    @pl.when((step == steps - 1) & (head == local - 1))
    def _():
        gain_out[0] = jnp.broadcast_to(
            jnp.sum(gain_acc[...], axis=1, keepdims=True), gain_out.shape[1:]
        )


def attention_specs(block, group_rows, local, spans):
    width = GROUP_HEADS * HEAD_SIZE
    tables = [
        pl.BlockSpec((1, block), lambda h, s, low, order: (0, s)),
        pl.BlockSpec((HALF, group_rows), lambda h, s, low, order: (0, 0)),
        pl.BlockSpec((HALF, group_rows), lambda h, s, low, order: (0, 0)),
        pl.BlockSpec((2, HEAD_SIZE, 1), lambda h, s, low, order: (0, 0, 0)),
    ]
    q_block = pl.BlockSpec((width, block), lambda h, s, low, order: (h, s))
    k_block = pl.BlockSpec((HEAD_SIZE, group_rows), lambda h, s, low, order: (h, 0))
    raw_q = pl.BlockSpec(
        (1, width, block), lambda h, s, low, order: (order[s // spans], h, s % spans)
    )
    ranks, token_rows = group_rows // (spans * block), spans * block
    raw_k = pl.BlockSpec(
        (ranks, HEAD_SIZE, token_rows),
        lambda h, s, low, order: (0, local * GROUP_HEADS + h, 0),
    )
    raw_v = pl.BlockSpec(
        (ranks, HEAD_SIZE, token_rows),
        lambda h, s, low, order: (0, local * (GROUP_HEADS + 1) + h, 0),
    )
    lse = pl.BlockSpec((1, 8, block), lambda h, s, low, order: (h, 0, s))
    return tables, q_block, k_block, raw_q, raw_k, raw_v, lse


def attend(qkv_raw, low, order, starts, cosine, sine, gains, ranks, local, block):
    token_rows = qkv_raw.shape[2]
    group_rows = token_rows * ranks
    spans = token_rows // block
    width = GROUP_HEADS * HEAD_SIZE
    tables, q_block, k_block, raw_q, raw_k, raw_v, lse = attention_specs(
        block, group_rows, local, spans
    )
    return pl.pallas_call(
        functools.partial(attend_kernel, block),
        out_shape=(
            jax.ShapeDtypeStruct((ranks, local * width, token_rows), BF16),
            jax.ShapeDtypeStruct((local * width, group_rows), BF16),
            jax.ShapeDtypeStruct((local * HEAD_SIZE, group_rows), BF16),
            jax.ShapeDtypeStruct((local * HEAD_SIZE, group_rows), BF16),
            jax.ShapeDtypeStruct((local, 8, group_rows), F32),
        ),
        grid_spec=pltpu.PrefetchScalarGridSpec(
            num_scalar_prefetch=2,
            grid=(local, group_rows // block),
            in_specs=[raw_q, raw_k, raw_v, *tables],
            out_specs=[raw_q, q_block, k_block, k_block, lse],
            scratch_shapes=[
                pltpu.VMEM((group_rows, HEAD_SIZE), BF16),
                pltpu.VMEM((width, block), F32),
                pltpu.VMEM((8, block), F32),
            ],
        ),
        compiler_params=pltpu.CompilerParams(vmem_limit_bytes=40 << 20),
        cost_estimate=pl.CostEstimate(
            flops=20 * local * width * group_rows * group_rows,
            bytes_accessed=12 * local * width * group_rows,
            transcendentals=local * GROUP_HEADS * group_rows * group_rows,
        ),
        name="attend",
    )(low, order, qkv_raw, qkv_raw, qkv_raw, starts, cosine, sine, gains)


def attend_back(
    qkv_raw, low, order, starts, cosine, sine, gains, query, key, value, lse_table, attended, grad,
    ranks, local, block,
):
    token_rows = qkv_raw.shape[2]
    group_rows = token_rows * ranks
    spans = token_rows // block
    width = GROUP_HEADS * HEAD_SIZE
    total = local * (width + 2 * HEAD_SIZE)
    tables, q_block, k_block, raw_q, raw_k, _, lse = attention_specs(
        block, group_rows, local, spans
    )
    return pl.pallas_call(
        functools.partial(attend_back_kernel, block, spans),
        out_shape=(
            jax.ShapeDtypeStruct((ranks, total, token_rows), BF16),
            jax.ShapeDtypeStruct((2, HEAD_SIZE, 128), F32),
        ),
        grid_spec=pltpu.PrefetchScalarGridSpec(
            num_scalar_prefetch=2,
            grid=(local, group_rows // block),
            in_specs=[
                raw_q, raw_k, *tables, q_block, k_block, k_block, lse, raw_q, raw_q,
            ],
            out_specs=[
                pl.BlockSpec((ranks, total, token_rows), lambda h, s, low, order: (0, 0, 0)),
                pl.BlockSpec((2, HEAD_SIZE, 128), lambda h, s, low, order: (0, 0, 0)),
            ],
            scratch_shapes=[
                pltpu.VMEM((group_rows, HEAD_SIZE), BF16),
                pltpu.VMEM((group_rows, HEAD_SIZE), BF16),
                pltpu.VMEM((width, block), F32),
                pltpu.VMEM((HEAD_SIZE, group_rows), F32),
                pltpu.VMEM((HEAD_SIZE, group_rows), F32),
                pltpu.VMEM((HEAD_SIZE, block), F32),
            ],
        ),
        compiler_params=pltpu.CompilerParams(vmem_limit_bytes=48 << 20),
        cost_estimate=pl.CostEstimate(
            flops=27 * local * width * group_rows * group_rows,
            bytes_accessed=16 * local * width * group_rows,
            transcendentals=local * GROUP_HEADS * group_rows * group_rows,
        ),
        name="attend_back",
    )(
        low, order, qkv_raw, qkv_raw, starts, cosine, sine, gains, query, key, value, lse_table,
        attended, grad,
    )


def rms_parts(rows, gain):
    scale = lax.rsqrt(jnp.mean(rows * rows, axis=-1, keepdims=True) + EPS)
    return scale, (rows * scale * gain).astype(BF16)


def rms_back(rows, scale, gain, grad):
    unit = rows * scale
    weighted = grad * gain
    row_grad = scale * (weighted - unit * jnp.mean(weighted * unit, axis=-1, keepdims=True))
    return row_grad, jnp.sum(grad * unit, axis=0)


def hop(rows, distance, ranks):
    return lax.ppermute(rows, "seq", [(i, i ^ distance) for i in range(ranks)])


def after(values, *first):
    return lax.optimization_barrier((values, first))[0]


def gather_chunks(rows, ranks):
    half = rows.shape[0] // 2
    if ranks != 4:
        moved = [rows] + [hop(rows, k, ranks) for k in range(1, ranks)]
        return [(m[:half], m[half:]) for m in moved]
    first, second = hop(rows, 1, ranks), hop(rows, 2, ranks)
    corner = hop(first[:half], 2, ranks), hop(second[half:], 1, ranks)
    return [(m[:half], m[half:]) for m in (rows, first, second)] + [corner]


def scatter_chunks(make, given, ranks, early=((), None), late=((), None)):
    def run(work, arrays):
        return work[1](arrays) if work[1] else ()

    if ranks != 4:
        sent = [make(k, given) for k in range(1, ranks)]
        sent, first, second = lax.optimization_barrier((sent, early[0], late[0]))
        own = make(0, given)
        more = run(early, first), run(late, second)
        moved = [hop(part, k + 1, ranks) for k, part in enumerate(sent)]
        moved, own, more = lax.optimization_barrier((moved, own, more))
        return sum((m.astype(F32) for m in moved), own.astype(F32)), *more
    corner = make(3, given)
    half = corner.shape[0] // 2
    corner, given, arrays = lax.optimization_barrier((corner, given, early[0]))
    for_second = hop(corner[:half], 1, ranks)
    for_first = hop(corner[half:], 2, ranks)
    first, second, early = make(1, given), make(2, given), run(early, arrays)

    def add(a, b):
        return (a.astype(F32) + b.astype(F32)).astype(BF16)

    first = jnp.concatenate([first[:half], add(first[half:], for_first)])
    second = jnp.concatenate([add(second[:half], for_second), second[half:]])
    first, second, given, early, arrays = lax.optimization_barrier(
        (first, second, given, early, late[0])
    )
    own, late = make(0, given), run(late, arrays)
    first, second, own, late = lax.optimization_barrier(
        (hop(first, 1, ranks), hop(second, 2, ranks), own, late)
    )
    return own.astype(F32) + first.astype(F32) + second.astype(F32), early, late


def up_kernel(tile, xa, xb, w_ref, *rest):
    f_ref, hid_ref, x_ref, x_all = rest[-4:]
    half = xa.shape[0]

    @pl.when(pl.program_id(0) == 0)
    def _():
        x_all[:half, :] = xa[...]
        x_all[half:, :] = xb[...]
        x_ref[...] = x_all[...]

    for i in range(w_ref.shape[1] // (2 * tile)):
        left, right = 2 * i * tile, (2 * i + 1) * tile
        both = dot(x_all[...], w_ref[:, left : left + 2 * tile], 1, 0)
        gate, up = both[:, :tile], both[:, tile:]
        gated = jax.nn.sigmoid(gate)
        silu = gate * gated
        hid_ref[:, i * tile : (i + 1) * tile] = (silu * up).astype(BF16)
        f_ref[:, left:right] = up * (gated + silu * (1.0 - gated))
        f_ref[:, right : right + tile] = silu


def up_chunk(k, x, gate_up, before, ranks, tile):
    half, features = x[0].shape
    rows, width = 2 * half, gate_up.shape[1]
    halves = [pl.BlockSpec((half, features), lambda t: (0, 0))] * 2
    step = min(2 * tile, width // 2)
    kept = [] if before is None else list(before)
    return pl.pallas_call(
        functools.partial(up_kernel, tile),
        out_shape=(
            jax.ShapeDtypeStruct((ranks * rows, width), F32),
            jax.ShapeDtypeStruct((ranks * rows, width // 2), BF16),
            jax.ShapeDtypeStruct((ranks * rows, features), BF16),
        ),
        grid=(width // (2 * step),),
        in_specs=halves
        + [pl.BlockSpec((features, 2 * step), lambda t: (0, t))]
        + [pl.BlockSpec(memory_space=pl.ANY)] * len(kept),
        out_specs=(
            pl.BlockSpec((rows, 2 * step), lambda t: (k, t)),
            pl.BlockSpec((rows, step), lambda t: (k, t)),
            pl.BlockSpec((rows, features), lambda t: (k, 0)),
        ),
        scratch_shapes=[pltpu.VMEM((rows, features), BF16)],
        input_output_aliases={3 + i: i for i in range(len(kept))},
        compiler_params=pltpu.CompilerParams(vmem_limit_bytes=48 << 20),
        cost_estimate=pl.CostEstimate(
            flops=3 * rows * features * width,
            bytes_accessed=2 * features * width + 5 * rows * width + 4 * rows * features,
            transcendentals=rows * width // 2,
        ),
        name="up_chunk",
    )(*x, gate_up, *kept)


def hidden_back_kernel(tile, c_ref, w_ref, f_ref, d_ref):
    for i in range(w_ref.shape[1] // tile):
        left, right = 2 * i * tile, (2 * i + 1) * tile
        hidden_grad = dot(c_ref[...], w_ref[:, i * tile : (i + 1) * tile], 1, 0)
        d_ref[:, left:right] = (hidden_grad * f_ref[:, left:right]).astype(BF16)
        d_ref[:, right : right + tile] = (hidden_grad * f_ref[:, right : right + tile]).astype(BF16)


def hidden_back(cot, down, factors, tile, rows):
    group_rows, features = cot.shape
    width = down.shape[1]
    step = min(2 * tile, width)
    return pl.pallas_call(
        functools.partial(hidden_back_kernel, tile),
        out_shape=jax.ShapeDtypeStruct((group_rows, 2 * width), BF16),
        grid=(group_rows // rows, width // step),
        in_specs=[
            pl.BlockSpec((rows, features), lambda r, t: (r, 0)),
            pl.BlockSpec((features, step), lambda r, t: (0, t)),
            pl.BlockSpec((rows, 2 * step), lambda r, t: (r, t)),
        ],
        out_specs=pl.BlockSpec((rows, 2 * step), lambda r, t: (r, t)),
        compiler_params=pltpu.CompilerParams(vmem_limit_bytes=48 << 20),
        cost_estimate=pl.CostEstimate(
            flops=3 * group_rows * features * width,
            bytes_accessed=4 * features * width + 12 * group_rows * width,
            transcendentals=group_rows * width,
        ),
        name="hidden_back",
    )(cot, down, factors)


def widen(pieces, place, columns, part, total, ranks):
    rows = 2 * pieces[0][0][0].shape[0]
    each = sum(stop - start for start, stop in columns)
    width = each * len(pieces)
    if ranks != 4:

        def picked(chunk):
            return jnp.concatenate([chunk[:, a:b] for a, b in columns], axis=1)

        stacked = jnp.stack(
            [
                jnp.concatenate(
                    [jnp.concatenate([picked(p) for p in group[k]]) for group in pieces], axis=1
                )
                for k in range(ranks)
            ]
        )
        ordered = jnp.swapaxes(jnp.take(stacked, place, axis=0), 0, 1)
        return ordered.reshape(rows, ranks * width).astype(F32)
    half = rows // 2
    flat = [p for group in pieces for chunk in group for p in chunk]
    counts = len(pieces)
    whole = pl.BlockSpec((half, part), lambda k, place: (0, total))

    def kernel(place_ref, *refs):
        out = refs[-1]
        for k in range(ranks):

            @pl.when(pl.program_id(0) == k)
            def _(k=k):
                at = 0
                for group in range(counts):
                    for start, stop in columns:
                        for side in range(2):
                            source = refs[(group * ranks + k) * 2 + side]
                            out[side * half : (side + 1) * half, at : at + stop - start] = source[
                                :, start:stop
                            ].astype(F32)
                        at += stop - start

    return pl.pallas_call(
        kernel,
        out_shape=jax.ShapeDtypeStruct((rows, ranks * width), F32),
        grid_spec=pltpu.PrefetchScalarGridSpec(
            num_scalar_prefetch=1,
            grid=(ranks,),
            in_specs=[whole] * len(flat),
            out_specs=pl.BlockSpec((rows, width), lambda k, place: (0, place[k])),
        ),
        compiler_params=pltpu.CompilerParams(vmem_limit_bytes=48 << 20),
        cost_estimate=pl.CostEstimate(
            flops=rows * width * ranks, bytes_accessed=6 * rows * width * ranks, transcendentals=0
        ),
        name="widen",
    )(place, *flat)


def body(
    tokens, mixed_cotangent, lengths, owner_slot, q_weight, key_projection, value_projection,
    out_weight, gate_weight, up_weight, down_weight, attn_gain, ffn_gain, query_gain, key_gain,
):
    groups = lax.axis_size("fsdp")
    ranks = lax.axis_size("seq")
    seq_index = lax.axis_index("seq")
    token_rows, features = tokens.shape
    slice_rows = token_rows // groups
    group_rows = token_rows * ranks
    local = KEY_VALUE_HEADS // ranks
    q_part = q_weight.shape[1] // ranks
    k_part = key_projection.shape[1] // ranks
    f_part = gate_weight.shape[1] // ranks
    h_part = q_part + 2 * k_part
    block = min(256, token_rows)
    tile = min(256, f_part)
    gain_rows = attn_gain.shape[0]

    local_slot = owner_slot % token_rows
    target = owner_slot // token_rows // ranks
    send_spot = target * slice_rows + local_slot % slice_rows
    inverse = (
        jnp.zeros((token_rows,), jnp.int32)
        .at[send_spot]
        .set(jnp.arange(token_rows, dtype=jnp.int32))
    )

    def exchange(rows):
        return lax.all_to_all(rows, "fsdp", split_axis=0, concat_axis=0, tiled=True)

    both_gains = jnp.concatenate([attn_gain, ffn_gain])
    gains_full = exchange(jnp.broadcast_to(both_gains, (groups, 2 * gain_rows))).astype(F32)
    attn_full = gains_full[:, :gain_rows].reshape(features)
    ffn_full = gains_full[:, gain_rows:].reshape(features)
    owned = exchange(tokens[inverse])

    def columns(weight, width):
        return lax.dynamic_slice_in_dim(weight, seq_index * width, width, 1)

    def gather(weight):
        return lax.all_gather(weight, "fsdp", axis=0, tiled=True)

    head_shard = (
        jnp.concatenate(
            [
                columns(q_weight, q_part),
                columns(key_projection, k_part),
                columns(value_projection, k_part),
                columns(out_weight, q_part),
            ],
            axis=1,
        )
    )

    def tiles(weight):
        return columns(weight, f_part).reshape(-1, f_part // tile, tile)

    gate_up_shard = jnp.concatenate([tiles(gate_weight), tiles(up_weight)], axis=2)
    owned, cot_rows, head_shard, gate_up_shard, down_shard = lax.optimization_barrier(
        (
            owned,
            mixed_cotangent[inverse],
            head_shard,
            gate_up_shard.reshape(-1, 2 * f_part),
            columns(down_weight, f_part),
        )
    )
    head_own = gather(head_shard)
    qkv_own, wo_own = head_own[:, :h_part], head_own[:, h_part:]
    gate_up_own = gather(gate_up_shard)
    down_own = gather(down_shard)
    cot_owned = exchange(cot_rows)

    lengths_row = lengths[0]
    token_spots = jnp.arange(group_rows, dtype=jnp.int32)
    seq_ends = jnp.cumsum(lengths_row)
    passed = token_spots[:, None] >= seq_ends[None, :]
    starts = jnp.sum(jnp.where(passed, lengths_row[None, :], 0), axis=1).astype(jnp.int32)
    places = (token_spots - starts).astype(F32)
    freqs = jnp.exp(jnp.arange(HALF, dtype=F32) * (-2.0 * math.log(THETA) / HEAD_SIZE))
    angles = freqs[:, None] * places[None, :]
    cosine, sine = jnp.cos(angles), jnp.sin(angles)
    low = starts[::block] // block
    start_row = starts[None, :]
    head_gains = jnp.stack([query_gain, key_gain]).astype(F32)[:, :, None]
    place = jnp.bitwise_xor(seq_index, jnp.arange(ranks, dtype=jnp.int32)).astype(jnp.int32)

    def together(chunks):
        return jnp.stack([jnp.concatenate(pair) for pair in chunks])

    tok_f32 = owned.astype(F32)
    scale_one, normed_own = rms_parts(tok_f32, attn_full)
    normed = gather_chunks(normed_own, ranks)
    normed[-1], cot_sent = lax.optimization_barrier((normed[-1], cot_owned))
    cot = gather_chunks(cot_sent, ranks)
    normed = together(normed)
    qkv_raw = jnp.stack([dot(qkv_own, normed[k], 0, 1) for k in range(ranks)])
    attended, query, key, value, lse_table = attend(
        qkv_raw, low, place, start_row, cosine, sine, head_gains, ranks, local, block
    )
    branch_sum, cot, _ = scatter_chunks(
        lambda k, given: dot(given[0][k], given[1], 0, 1).astype(BF16),
        (after(attended, cot[:3]), wo_own),
        ranks,
        early=(cot, together),
    )
    resid = tok_f32 + branch_sum

    scale_two, normed_two_own = rms_parts(resid, ffn_full)
    results = None
    for k, chunk in enumerate(gather_chunks(normed_two_own, ranks)):
        results = up_chunk(k, chunk, gate_up_own, results, ranks, tile)
    factors, hidden, normed_two = results
    cot = cot.reshape(group_rows, features)
    gate_up_grad = hidden_back(cot, down_own, factors, tile, token_rows)

    def rows_of(array, k):
        return array[k * token_rows : (k + 1) * token_rows]

    def scatter(terms):
        return lax.psum_scatter(
            terms.astype(BF16), "fsdp", scatter_dimension=0, tiled=True
        )

    def terms_of(left, right):
        return dot(left, right, 0, 0).astype(BF16)

    down_terms = terms_of(cot, hidden)
    normed_two_grad, _, left_terms = scatter_chunks(
        lambda k, given: dot(rows_of(given[0], k), given[1], 1, 1).astype(BF16),
        (gate_up_grad, gate_up_own),
        ranks,
        late=(normed_two, lambda rows: terms_of(rows, gate_up_grad[:, :f_part])),
    )
    down_grad = scatter(down_terms)
    left_grad = scatter(left_terms)
    resid_part, ffn_gain_part = rms_back(resid, scale_two, ffn_full, normed_two_grad)
    resid_grad = cot_owned.astype(F32) + resid_part
    branch_own = resid_grad.astype(BF16)
    branch_own, right_in, hidden = lax.optimization_barrier((branch_own, normed_two, hidden))
    branch = gather_chunks(branch_own, ranks)
    right_terms = terms_of(right_in, gate_up_grad[:, f_part:])
    down_parts = jnp.stack(
        [
            dot(
                lax.dynamic_slice_in_dim(hidden, place[j] * token_rows, token_rows, 0),
                down_own, 1, 1,
            ).astype(BF16)
            for j in range(ranks)
        ]
    )
    branch[-1], right_terms, down_parts = lax.optimization_barrier(
        (branch[-1], right_terms, down_parts)
    )
    branch = together(branch)
    right_grad = scatter(right_terms)
    attended_grad = jnp.stack(
        [dot(wo_own, branch[k], 0, 1).astype(BF16) for k in range(ranks)]
    )
    d_heads, head_gain_parts = attend_back(
        qkv_raw, low, place, start_row, cosine, sine, head_gains, query, key, value, lse_table,
        attended, after(attended_grad, down_grad), ranks, local, block,
    )
    down_moved = lax.all_to_all(down_parts, "seq", split_axis=0, concat_axis=0, tiled=True)
    d_heads = after(d_heads, left_grad)

    def outer(left, right):
        return lax.dot_general(
            left.reshape(ranks, token_rows, features), right,
            (((0, 1), (0, 2)), ((), ())), preferred_element_type=F32,
        ).astype(BF16)

    normed_grad, head_terms, mixed_own = scatter_chunks(
        lambda k, given: dot(given[0][k], given[1], 0, 1).astype(BF16),
        (d_heads, qkv_own),
        ranks,
        early=(
            (d_heads, attended),
            lambda a: jnp.concatenate([outer(normed, a[0]), outer(branch, a[1])], axis=1),
        ),
        late=(down_moved, lambda a: (resid + jnp.sum(a.astype(F32), axis=0)).astype(BF16)),
    )
    head_grad = scatter(head_terms)
    back_mixed = exchange(mixed_own)
    tok_part, attn_gain_part = rms_back(tok_f32, scale_one, attn_full, normed_grad)
    input_grad_own = after((resid_grad + tok_part).astype(BF16), right_grad, back_mixed)
    back_grad = exchange(input_grad_own)

    down_all = gather_chunks(down_grad, ranks)
    left_all = gather_chunks(left_grad, ranks)
    right_all = gather_chunks(right_grad, ranks)
    head_all = gather_chunks(head_grad, ranks)

    packed = jnp.concatenate(
        [
            attn_gain_part.reshape(groups, -1),
            ffn_gain_part.reshape(groups, -1),
            jnp.broadcast_to(head_gain_parts[0, :, 0], (groups, HEAD_SIZE)),
            jnp.broadcast_to(head_gain_parts[1, :, 0], (groups, HEAD_SIZE)),
        ],
        axis=1,
    )
    summed = jnp.sum(exchange(packed), axis=0)
    summed = jnp.sum(lax.all_gather(summed, "seq", axis=0, tiled=False), axis=0)

    def of_heads(start, width):
        return widen([head_all], place, [(0, width)], width, start // width, ranks)

    def of_tiles(side):
        spans = [(at + side * tile, at + (side + 1) * tile) for at in range(0, f_part, 2 * tile)]
        return widen([left_all, right_all], place, spans, f_part, 0, ranks)

    return (
        back_mixed[send_spot],
        back_grad[send_spot],
        of_heads(0, q_part),
        of_heads(q_part, k_part),
        of_heads(q_part + k_part, k_part),
        widen([head_all], place, [(h_part, h_part + q_part)], h_part + q_part, 0, ranks),
        of_tiles(0),
        of_tiles(1),
        widen([down_all], place, [(0, f_part)], f_part, 0, ranks),
        summed[:gain_rows],
        summed[gain_rows : 2 * gain_rows],
        summed[2 * gain_rows : 2 * gain_rows + HEAD_SIZE],
        summed[2 * gain_rows + HEAD_SIZE :],
    )


def solution(mesh):
    rows = P("fsdp", None)
    tokens = P(("fsdp", "seq"), None)
    in_specs = (
        tokens, tokens, rows, P(("fsdp", "seq")), rows, rows, rows, rows, rows, rows, rows,
        P("fsdp"), P("fsdp"), P(), P(),
    )
    out_specs = (
        tokens, tokens, rows, rows, rows, rows, rows, rows, rows,
        P("fsdp"), P("fsdp"), P(), P(),
    )
    return jax.shard_map(body, mesh=mesh, in_specs=in_specs, out_specs=out_specs, check_vma=False)
```

```python
import functools
import math

import jax
import jax.numpy as jnp
from jax import lax
from jax.experimental import pallas as pl
from jax.experimental.pallas import tpu as pltpu
from jax.sharding import PartitionSpec as P

QUERY_HEADS = 32
KEY_VALUE_HEADS = 8
HEAD_SIZE = 64
HALF = HEAD_SIZE // 2
GROUP_HEADS = QUERY_HEADS // KEY_VALUE_HEADS

EPS = 1e-05
THETA = 1000000.0
SCALE = 1.0 / math.sqrt(HEAD_SIZE)
LOG2E = math.log2(math.e)
F32 = jnp.float32
BF16 = jnp.bfloat16


def dot(left, right, left_dim, right_dim):
    return lax.dot_general(
        left, right, (((left_dim,), (right_dim,)), ((), ())), preferred_element_type=F32
    )


def rms_rope(raw, gain, cosine, sine):
    normed = raw * lax.rsqrt(jnp.mean(raw * raw, axis=0, keepdims=True) + EPS) * gain
    first, second = normed[:HALF], normed[HALF:]
    return jnp.concatenate(
        [first * cosine - second * sine, second * cosine + first * sine], axis=0
    )


def rms_rope_back(raw, gain, cosine, sine, grad):
    first, second = grad[:HALF], grad[HALF:]
    turned = jnp.concatenate(
        [first * cosine + second * sine, second * cosine - first * sine], axis=0
    )
    scale = lax.rsqrt(jnp.mean(raw * raw, axis=0, keepdims=True) + EPS)
    unit = raw * scale
    weighted = gain * turned
    raw_grad = scale * (weighted - unit * jnp.mean(weighted * unit, axis=0, keepdims=True))
    return raw_grad, turned * unit


def attend_kernel(
    block, low_ref, order_ref, q_raw, k_raw, v_raw, start_ref, cos_ref, sin_ref, gains_ref,
    out_ref, q_out, k_out, v_out, lse_ref, k_rows, acc, total,
):
    step = pl.program_id(1)
    query_gain, key_gain = gains_ref[0], gains_ref[1]

    @pl.when(step == 0)
    def _():
        token_rows = k_raw.shape[2]
        for r in range(k_raw.shape[0]):
            part = slice(r * token_rows, (r + 1) * token_rows)
            at = order_ref[r]
            key = rms_rope(k_raw[at], key_gain, cos_ref[:, part], sin_ref[:, part])
            k_out[:, part] = key.astype(BF16)
            k_rows[part, :] = key.T.astype(BF16)
            v_out[:, part] = v_raw[at].astype(BF16)

    columns = pl.ds(pl.multiple_of(step * block, block), block)
    cosine, sine = cos_ref[:, columns], sin_ref[:, columns]
    for g in range(GROUP_HEADS):
        rows = slice(g * HEAD_SIZE, (g + 1) * HEAD_SIZE)
        q_out[rows, :] = rms_rope(q_raw[0, rows, :], query_gain, cosine, sine).astype(BF16)
    acc[...] = jnp.zeros_like(acc)
    total[...] = jnp.zeros_like(total)
    starts = start_ref[...]
    spots = step * block + lax.broadcasted_iota(jnp.int32, (1, block), 1)

    def inner(j, carry):
        keys = pl.ds(pl.multiple_of(j * block, block), block)
        key_rows = k_rows[keys, :]
        value = v_out[:, keys]
        key_spots = j * block + lax.broadcasted_iota(jnp.int32, (block, 1), 0)
        allowed = (key_spots >= starts) & (key_spots <= spots)
        for g in range(GROUP_HEADS):
            rows = slice(g * HEAD_SIZE, (g + 1) * HEAD_SIZE)
            score = dot(key_rows, q_out[rows, :], 1, 0)
            prob = jnp.where(allowed, jnp.exp2(score * (SCALE * LOG2E)), 0.0)
            total[g : g + 1, :] += jnp.sum(prob, axis=0, keepdims=True)
            acc[rows, :] += dot(value, prob.astype(BF16), 1, 0)
        return carry

    lax.fori_loop(low_ref[step], step + 1, inner, 0)
    for g in range(GROUP_HEADS):
        rows = slice(g * HEAD_SIZE, (g + 1) * HEAD_SIZE)
        summed = total[g : g + 1, :]
        out_ref[0, rows, :] = (acc[rows, :] / summed).astype(BF16)
        lse_ref[0, g : g + 1, :] = jnp.log2(summed)


def attend_back_kernel(
    block, spans, low_ref, order_ref, q_raw, k_raw, start_ref, cos_ref, sin_ref, gains_ref,
    q_ref, k_ref, v_ref, lse_ref, out_ref, grad_ref,
    d_ref, gain_out, k_rows, v_rows, dq, dk, dv, gain_acc,
):
    head, step = pl.program_id(0), pl.program_id(1)
    steps = pl.num_programs(1)
    local = pl.num_programs(0)
    query_gain, key_gain = gains_ref[0], gains_ref[1]
    width = GROUP_HEADS * HEAD_SIZE
    token_rows = spans * block

    @pl.when((head == 0) & (step == 0))
    def _():
        gain_acc[...] = jnp.zeros_like(gain_acc)
        gain_out[...] = jnp.zeros_like(gain_out)

    @pl.when(step == 0)
    def _():
        k_rows[...] = k_ref[...].astype(F32).T.astype(BF16)
        v_rows[...] = v_ref[...].astype(F32).T.astype(BF16)
        dk[...] = jnp.zeros_like(dk)
        dv[...] = jnp.zeros_like(dv)

    columns = pl.ds(pl.multiple_of(step * block, block), block)
    cosine, sine = cos_ref[:, columns], sin_ref[:, columns]
    dq[...] = jnp.zeros_like(dq)
    starts = start_ref[...]
    spots = step * block + lax.broadcasted_iota(jnp.int32, (1, block), 1)
    inner_sums = [
        jnp.sum(
            out_ref[0, g * HEAD_SIZE : (g + 1) * HEAD_SIZE, :].astype(F32)
            * grad_ref[0, g * HEAD_SIZE : (g + 1) * HEAD_SIZE, :].astype(F32),
            axis=0,
            keepdims=True,
        )
        for g in range(GROUP_HEADS)
    ]

    def inner(j, carry):
        keys = pl.ds(pl.multiple_of(j * block, block), block)
        key_rows, value_rows, key = k_rows[keys, :], v_rows[keys, :], k_ref[:, keys]
        key_spots = j * block + lax.broadcasted_iota(jnp.int32, (block, 1), 0)
        allowed = (key_spots >= starts) & (key_spots <= spots)
        key_sum = jnp.zeros((HEAD_SIZE, block), F32)
        value_sum = jnp.zeros((HEAD_SIZE, block), F32)
        for g in range(GROUP_HEADS):
            rows = slice(g * HEAD_SIZE, (g + 1) * HEAD_SIZE)
            query, grad = q_ref[rows, :], grad_ref[0, rows, :]
            score = dot(key_rows, query, 1, 0) * (SCALE * LOG2E) - lse_ref[0, g : g + 1, :]
            prob = jnp.where(allowed, jnp.exp2(score), 0.0)
            prob_grad = dot(value_rows, grad, 1, 0)
            score_grad = (prob * (prob_grad - inner_sums[g])).astype(BF16)
            value_sum += dot(grad, prob.astype(BF16), 1, 1)
            key_sum += dot(query, score_grad, 1, 1)
            dq[rows, :] += dot(key, score_grad, 1, 0)
        dk[:, keys] += key_sum
        dv[:, keys] += value_sum
        return carry

    lax.fori_loop(low_ref[step], step + 1, inner, 0)
    span = step // spans
    inside = pl.ds(pl.multiple_of((step % spans) * block, block), block)
    for g in range(GROUP_HEADS):
        rows = slice(g * HEAD_SIZE, (g + 1) * HEAD_SIZE)
        grad = (dq[rows, :] * SCALE).astype(BF16).astype(F32)
        raw_grad, terms = rms_rope_back(q_raw[0, rows, :], query_gain, cosine, sine, grad)
        d_ref[order_ref[span], pl.ds(pl.multiple_of(head * width + g * HEAD_SIZE, HEAD_SIZE), HEAD_SIZE), inside] = (
            raw_grad.astype(BF16)
        )
        gain_acc[...] += terms

    @pl.when(step == steps - 1)
    def _():
        key_at = pl.ds(pl.multiple_of(local * width + head * HEAD_SIZE, HEAD_SIZE), HEAD_SIZE)
        value_at = pl.ds(
            pl.multiple_of(local * (width + HEAD_SIZE) + head * HEAD_SIZE, HEAD_SIZE), HEAD_SIZE
        )
        for r in range(d_ref.shape[0]):
            part = slice(r * token_rows, (r + 1) * token_rows)
            grad = (dk[:, part] * SCALE).astype(BF16).astype(F32)
            raw_grad, terms = rms_rope_back(
                k_raw[order_ref[r]], key_gain, cos_ref[:, part], sin_ref[:, part], grad
            )
            d_ref[order_ref[r], key_at, :] = raw_grad.astype(BF16)
            d_ref[order_ref[r], value_at, :] = dv[:, part].astype(BF16)
            gain_out[1] += jnp.broadcast_to(
                jnp.sum(terms, axis=1, keepdims=True), gain_out.shape[1:]
            )

    @pl.when((step == steps - 1) & (head == local - 1))
    def _():
        gain_out[0] = jnp.broadcast_to(
            jnp.sum(gain_acc[...], axis=1, keepdims=True), gain_out.shape[1:]
        )


def attention_specs(block, group_rows, local, spans):
    width = GROUP_HEADS * HEAD_SIZE
    tables = [
        pl.BlockSpec((1, block), lambda h, s, low, order: (0, s)),
        pl.BlockSpec((HALF, group_rows), lambda h, s, low, order: (0, 0)),
        pl.BlockSpec((HALF, group_rows), lambda h, s, low, order: (0, 0)),
        pl.BlockSpec((2, HEAD_SIZE, 1), lambda h, s, low, order: (0, 0, 0)),
    ]
    q_block = pl.BlockSpec((width, block), lambda h, s, low, order: (h, s))
    k_block = pl.BlockSpec((HEAD_SIZE, group_rows), lambda h, s, low, order: (h, 0))
    raw_q = pl.BlockSpec(
        (1, width, block), lambda h, s, low, order: (order[s // spans], h, s % spans)
    )
    ranks, token_rows = group_rows // (spans * block), spans * block
    raw_k = pl.BlockSpec(
        (ranks, HEAD_SIZE, token_rows),
        lambda h, s, low, order: (0, local * GROUP_HEADS + h, 0),
    )
    raw_v = pl.BlockSpec(
        (ranks, HEAD_SIZE, token_rows),
        lambda h, s, low, order: (0, local * (GROUP_HEADS + 1) + h, 0),
    )
    lse = pl.BlockSpec((1, 8, block), lambda h, s, low, order: (h, 0, s))
    return tables, q_block, k_block, raw_q, raw_k, raw_v, lse


def attend(qkv_raw, low, order, starts, cosine, sine, gains, ranks, local, block):
    token_rows = qkv_raw.shape[2]
    group_rows = token_rows * ranks
    spans = token_rows // block
    width = GROUP_HEADS * HEAD_SIZE
    tables, q_block, k_block, raw_q, raw_k, raw_v, lse = attention_specs(
        block, group_rows, local, spans
    )
    return pl.pallas_call(
        functools.partial(attend_kernel, block),
        out_shape=(
            jax.ShapeDtypeStruct((ranks, local * width, token_rows), BF16),
            jax.ShapeDtypeStruct((local * width, group_rows), BF16),
            jax.ShapeDtypeStruct((local * HEAD_SIZE, group_rows), BF16),
            jax.ShapeDtypeStruct((local * HEAD_SIZE, group_rows), BF16),
            jax.ShapeDtypeStruct((local, 8, group_rows), F32),
        ),
        grid_spec=pltpu.PrefetchScalarGridSpec(
            num_scalar_prefetch=2,
            grid=(local, group_rows // block),
            in_specs=[raw_q, raw_k, raw_v, *tables],
            out_specs=[raw_q, q_block, k_block, k_block, lse],
            scratch_shapes=[
                pltpu.VMEM((group_rows, HEAD_SIZE), BF16),
                pltpu.VMEM((width, block), F32),
                pltpu.VMEM((8, block), F32),
            ],
        ),
        compiler_params=pltpu.CompilerParams(vmem_limit_bytes=40 << 20),
        cost_estimate=pl.CostEstimate(flops=1 << 20, bytes_accessed=1 << 20, transcendentals=0),
        name="attend",
    )(low, order, qkv_raw, qkv_raw, qkv_raw, starts, cosine, sine, gains)


def attend_back(
    qkv_raw, low, order, starts, cosine, sine, gains, query, key, value, lse_table, attended, grad,
    ranks, local, block,
):
    token_rows = qkv_raw.shape[2]
    group_rows = token_rows * ranks
    spans = token_rows // block
    width = GROUP_HEADS * HEAD_SIZE
    total = local * (width + 2 * HEAD_SIZE)
    tables, q_block, k_block, raw_q, raw_k, _, lse = attention_specs(
        block, group_rows, local, spans
    )
    return pl.pallas_call(
        functools.partial(attend_back_kernel, block, spans),
        out_shape=(
            jax.ShapeDtypeStruct((ranks, total, token_rows), BF16),
            jax.ShapeDtypeStruct((2, HEAD_SIZE, 128), F32),
        ),
        grid_spec=pltpu.PrefetchScalarGridSpec(
            num_scalar_prefetch=2,
            grid=(local, group_rows // block),
            in_specs=[
                raw_q, raw_k, *tables, q_block, k_block, k_block, lse, raw_q, raw_q,
            ],
            out_specs=[
                pl.BlockSpec((ranks, total, token_rows), lambda h, s, low, order: (0, 0, 0)),
                pl.BlockSpec((2, HEAD_SIZE, 128), lambda h, s, low, order: (0, 0, 0)),
            ],
            scratch_shapes=[
                pltpu.VMEM((group_rows, HEAD_SIZE), BF16),
                pltpu.VMEM((group_rows, HEAD_SIZE), BF16),
                pltpu.VMEM((width, block), F32),
                pltpu.VMEM((HEAD_SIZE, group_rows), F32),
                pltpu.VMEM((HEAD_SIZE, group_rows), F32),
                pltpu.VMEM((HEAD_SIZE, block), F32),
            ],
        ),
        compiler_params=pltpu.CompilerParams(vmem_limit_bytes=48 << 20),
        cost_estimate=pl.CostEstimate(
            flops=400 * 10**9, bytes_accessed=1 << 20, transcendentals=0
        ),
        name="attend_back",
    )(
        low, order, qkv_raw, qkv_raw, starts, cosine, sine, gains, query, key, value, lse_table,
        attended, grad,
    )


def rms_parts(rows, gain):
    scale = lax.rsqrt(jnp.mean(rows * rows, axis=-1, keepdims=True) + EPS)
    return scale, (rows * scale * gain).astype(BF16)


def rms_back(rows, scale, gain, grad):
    unit = rows * scale
    weighted = grad * gain
    row_grad = scale * (weighted - unit * jnp.mean(weighted * unit, axis=-1, keepdims=True))
    return row_grad, jnp.sum(grad * unit, axis=0)


def hop(rows, distance, ranks):
    return lax.ppermute(rows, "seq", [(i, i ^ distance) for i in range(ranks)])


def after(values, *first):
    return lax.optimization_barrier((values, first))[0]


def gather_start(rows, ranks):
    return [rows] + [hop(rows, k, ranks) for k in range(1, ranks if ranks != 4 else 3)]


def gather_finish(chunks, ranks):
    half = chunks[0].shape[0] // 2
    pairs = [((m, 0), (m, 1)) for m in chunks]
    if ranks == 4:
        corner = hop(chunks[1][:half], 2, ranks), hop(chunks[2][half:], 1, ranks)
        pairs.append(((corner[0], 0), (corner[1], 0)))
    return pairs


def gather_chunks(rows, ranks):
    return gather_finish(gather_start(rows, ranks), ranks)


def joined(pair):
    (first, _), (second, _) = pair
    return first if first is second else jnp.concatenate([first, second])


def pieces_of(pairs):
    flat = [piece for pair in pairs for piece in pair]
    return [m for m, _ in flat], [at for _, at in flat]


def add(a, b):
    return (a.astype(F32) + b.astype(F32)).astype(BF16)


def scatter_chunks(make, given, ranks, early=((), None), late=((), None), keep=False, wait=()):
    def run(work, arrays):
        return work[1](arrays) if work[1] else ()

    if ranks != 4:
        sent = [make(k, given) for k in range(1, ranks)]
        sent, first, second = lax.optimization_barrier((sent, early[0], late[0]))
        own = make(0, given)
        more = run(early, first), run(late, second)
        moved = [hop(part, k + 1, ranks) for k, part in enumerate(sent)]
        moved, own, wait = lax.optimization_barrier((moved, own, wait))
        return sum((m.astype(F32) for m in moved), own.astype(F32)), *more, wait
    corner = make(3, given)
    half = corner.shape[0] // 2
    corner, given, arrays = lax.optimization_barrier((corner, given, early[0]))
    for_second = hop(corner[:half], 1, ranks)
    for_first = hop(corner[half:], 2, ranks)
    first = make(1, given)
    top = first[:half]
    top, given = lax.optimization_barrier((top, given))
    top = hop(top, 1, ranks)
    second, early = make(2, given), run(early, arrays)

    bottom = second[half:]
    first, second = add(first[half:], for_first), add(second[:half], for_second)
    bottom, first, second, given, early, arrays = lax.optimization_barrier(
        (bottom, first, second, given, early, late[0])
    )
    own, late = make(0, given), run(late, arrays)
    moved = top, hop(first, 1, ranks), hop(second, 2, ranks), hop(bottom, 2, ranks), own
    if keep:
        moved, wait = lax.optimization_barrier((moved, wait))
    else:
        moved, late, wait = lax.optimization_barrier((moved, late, wait))
    top, first, second, bottom, own = moved
    first = jnp.concatenate([top, first]).astype(F32)
    second = jnp.concatenate([second, bottom]).astype(F32)
    return own.astype(F32) + first + second, early, late, wait


def rows_kernel(left, right, out):
    out[...] = dot(left[...], right[...], 1, 1).astype(BF16)


def rows_times(left, k, right, rows):
    width, depth = right.shape
    tile = min(512, width)
    return pl.pallas_call(
        rows_kernel,
        out_shape=jax.ShapeDtypeStruct((rows, width), BF16),
        grid=(width // tile,),
        in_specs=[
            pl.BlockSpec((rows, depth), lambda t: (k, 0)),
            pl.BlockSpec((tile, depth), lambda t: (t, 0)),
        ],
        out_specs=pl.BlockSpec((rows, tile), lambda t: (0, t)),
        compiler_params=pltpu.CompilerParams(vmem_limit_bytes=48 << 20),
        cost_estimate=pl.CostEstimate(flops=1 << 20, bytes_accessed=1 << 20, transcendentals=0),
        name="rows_times",
    )(left, right)


def up_kernel(tile, xa, xb, w_ref, *rest):
    f_ref, hid_ref, x_ref, x_all = rest[-4:]
    half = xa.shape[0]

    @pl.when(pl.program_id(0) == 0)
    def _():
        x_all[:half, :] = xa[...]
        x_all[half:, :] = xb[...]
        x_ref[...] = x_all[...]

    for i in range(w_ref.shape[1] // (2 * tile)):
        left, right = 2 * i * tile, (2 * i + 1) * tile
        both = dot(x_all[...], w_ref[:, left : left + 2 * tile], 1, 0)
        gate, up = both[:, :tile], both[:, tile:]
        gated = jax.nn.sigmoid(gate)
        silu = gate * gated
        hid_ref[:, i * tile : (i + 1) * tile] = (silu * up).astype(BF16)
        f_ref[:, left:right] = (up * (gated + silu * (1.0 - gated))).astype(BF16)
        f_ref[:, right : right + tile] = silu.astype(BF16)


def up_chunk(k, x, gate_up, before, ranks, tile, rows):
    arrays, places = pieces_of([x])
    half, features = rows // 2, arrays[0].shape[1]
    width = gate_up.shape[1]
    halves = [pl.BlockSpec((half, features), lambda t, at=at: (at, 0)) for at in places]
    step = min(2 * tile, width // 2)
    kept = [] if before is None else list(before)
    return pl.pallas_call(
        functools.partial(up_kernel, tile),
        out_shape=(
            jax.ShapeDtypeStruct((ranks * rows, width), BF16),
            jax.ShapeDtypeStruct((ranks * rows, width // 2), BF16),
            jax.ShapeDtypeStruct((ranks * rows, features), BF16),
        ),
        grid=(width // (2 * step),),
        in_specs=halves
        + [pl.BlockSpec((features, 2 * step), lambda t: (0, t))]
        + [pl.BlockSpec(memory_space=pl.ANY)] * len(kept),
        out_specs=(
            pl.BlockSpec((rows, 2 * step), lambda t: (k, t)),
            pl.BlockSpec((rows, step), lambda t: (k, t)),
            pl.BlockSpec((rows, features), lambda t: (k, 0)),
        ),
        scratch_shapes=[pltpu.VMEM((rows, features), BF16)],
        input_output_aliases={3 + i: i for i in range(len(kept))},
        compiler_params=pltpu.CompilerParams(vmem_limit_bytes=48 << 20),
        cost_estimate=pl.CostEstimate(flops=1 << 20, bytes_accessed=1 << 20, transcendentals=0),
        name="up_chunk",
    )(*arrays, gate_up, *kept)


def head_outer_kernel(count, d_ref, a_ref, *refs):
    out = refs[-1]
    at = 0
    for left, pieces in ((d_ref, refs[:count]), (a_ref, refs[count : 2 * count])):
        half = pieces[0].shape[0]
        total = sum(
            dot(left[i // 2, :, (i % 2) * half : (i % 2 + 1) * half], piece[...], 1, 0)
            for i, piece in enumerate(pieces)
        )
        out[:, at : at + left.shape[1]] = total.T.astype(BF16)
        at += left.shape[1]


def head_outer(d_heads, normed, attended, branch):
    ranks, width, rows = d_heads.shape
    more = attended.shape[1]
    left, left_places = pieces_of(normed)
    right, right_places = pieces_of(branch)
    features = left[0].shape[1]
    tile = min(512, features)

    def heads(w):
        return pl.BlockSpec((ranks, w, rows), lambda t: (0, 0, 0))

    tokens = [
        pl.BlockSpec((rows // 2, tile), lambda t, at=at: (at, t))
        for at in left_places + right_places
    ]
    return pl.pallas_call(
        functools.partial(head_outer_kernel, len(left)),
        out_shape=jax.ShapeDtypeStruct((features, width + more), BF16),
        grid=(features // tile,),
        in_specs=[heads(width), heads(more), *tokens],
        out_specs=pl.BlockSpec((tile, width + more), lambda t: (t, 0)),
        compiler_params=pltpu.CompilerParams(vmem_limit_bytes=48 << 20),
        cost_estimate=pl.CostEstimate(flops=1 << 20, bytes_accessed=1 << 20, transcendentals=0),
        name="head_outer",
    )(d_heads, attended, *left, *right)


def hidden_back_kernel(tile, c_ref, w_ref, f_ref, d_ref):
    rows = c_ref.shape[0] // 4
    for r in range(4):
        at = slice(r * rows, (r + 1) * rows)
        hidden_grad = dot(c_ref[at, :], w_ref[...], 1, 0)
        for i in range(w_ref.shape[1] // tile):
            left, right = 2 * i * tile, (2 * i + 1) * tile
            part = hidden_grad[:, i * tile : (i + 1) * tile]
            d_ref[at, left:right] = (part * f_ref[at, left:right].astype(F32)).astype(BF16)
            d_ref[at, right : right + tile] = (
                part * f_ref[at, right : right + tile].astype(F32)
            ).astype(BF16)


def hidden_back(cot, down, factors, tile):
    group_rows, features = cot.shape
    width = down.shape[1]
    step = min(2 * tile, width)
    return pl.pallas_call(
        functools.partial(hidden_back_kernel, tile),
        out_shape=jax.ShapeDtypeStruct((group_rows, 2 * width), BF16),
        grid=(width // step,),
        in_specs=[
            pl.BlockSpec((group_rows, features), lambda t: (0, 0)),
            pl.BlockSpec((features, step), lambda t: (0, t)),
            pl.BlockSpec((group_rows, 2 * step), lambda t: (0, t)),
        ],
        out_specs=pl.BlockSpec((group_rows, 2 * step), lambda t: (0, t)),
        compiler_params=pltpu.CompilerParams(vmem_limit_bytes=56 << 20),
        cost_estimate=pl.CostEstimate(flops=1 << 20, bytes_accessed=1 << 20, transcendentals=0),
        name="hidden_back",
    )(cot, down, factors)


def widen(pieces, place, columns, part, total, ranks, rows):
    each = sum(stop - start for start, stop in columns)
    width = each * len(pieces)
    if ranks != 4:

        def picked(chunk):
            return jnp.concatenate([chunk[:, a:b] for a, b in columns], axis=1)

        stacked = jnp.stack(
            [
                jnp.concatenate(
                    [picked(joined(group[k])) for group in pieces], axis=1
                )
                for k in range(ranks)
            ]
        )
        ordered = jnp.swapaxes(jnp.take(stacked, place, axis=0), 0, 1)
        return ordered.reshape(rows, ranks * width).astype(F32)
    half = rows // 2
    flat, places = pieces_of([pair for group in pieces for pair in group])
    counts = len(pieces)
    whole = [
        pl.BlockSpec((half, part), lambda k, place, at=at: (at, total)) for at in places
    ]

    def kernel(place_ref, *refs):
        out = refs[-1]
        for k in range(ranks):

            @pl.when(pl.program_id(0) == k)
            def _(k=k):
                at = 0
                for group in range(counts):
                    for start, stop in columns:
                        for side in range(2):
                            source = refs[(group * ranks + k) * 2 + side]
                            out[side * half : (side + 1) * half, at : at + stop - start] = source[
                                :, start:stop
                            ].astype(F32)
                        at += stop - start

    return pl.pallas_call(
        kernel,
        out_shape=jax.ShapeDtypeStruct((rows, ranks * width), F32),
        grid_spec=pltpu.PrefetchScalarGridSpec(
            num_scalar_prefetch=1,
            grid=(ranks,),
            in_specs=whole,
            out_specs=pl.BlockSpec((rows, width), lambda k, place: (0, place[k])),
        ),
        compiler_params=pltpu.CompilerParams(vmem_limit_bytes=48 << 20),
        cost_estimate=pl.CostEstimate(
            flops=rows * width * ranks * 15000, bytes_accessed=1 << 20, transcendentals=0
        ),
        name="widen",
    )(place, *flat)


def body(
    tokens, mixed_cotangent, lengths, owner_slot, q_weight, key_projection, value_projection,
    out_weight, gate_weight, up_weight, down_weight, attn_gain, ffn_gain, query_gain, key_gain,
):
    groups = lax.axis_size("fsdp")
    ranks = lax.axis_size("seq")
    seq_index = lax.axis_index("seq")
    token_rows, features = tokens.shape
    slice_rows = token_rows // groups
    group_rows = token_rows * ranks
    local = KEY_VALUE_HEADS // ranks
    q_part = q_weight.shape[1] // ranks
    k_part = key_projection.shape[1] // ranks
    f_part = gate_weight.shape[1] // ranks
    h_part = q_part + 2 * k_part
    block = min(256, token_rows)
    tile = min(256, f_part)
    gain_rows = attn_gain.shape[0]
    shard = q_weight.shape[0]

    local_slot = owner_slot % token_rows
    target = owner_slot // token_rows // ranks
    send_spot = target * slice_rows + local_slot % slice_rows
    inverse = (
        jnp.zeros((token_rows,), jnp.int32)
        .at[send_spot]
        .set(jnp.arange(token_rows, dtype=jnp.int32))
    )

    def exchange(rows):
        return lax.all_to_all(rows, "fsdp", split_axis=0, concat_axis=0, tiled=True)

    both_gains = jnp.concatenate([attn_gain, ffn_gain])
    gains_full = exchange(jnp.broadcast_to(both_gains, (groups, 2 * gain_rows))).astype(F32)
    token_rows_sent, gains_full = lax.optimization_barrier((tokens[inverse], gains_full))
    owned = exchange(token_rows_sent)
    attn_full = gains_full[:, :gain_rows].reshape(features)
    ffn_full = gains_full[:, gain_rows:].reshape(features)

    def columns(weight, width):
        return lax.dynamic_slice_in_dim(weight, seq_index * width, width, 1)

    def gather(weight):
        return lax.all_gather(weight, "fsdp", axis=0, tiled=True)

    head_shard = (
        jnp.concatenate(
            [
                columns(q_weight, q_part),
                columns(key_projection, k_part),
                columns(value_projection, k_part),
                columns(out_weight, q_part),
            ],
            axis=1,
        )
    )

    def tiles(weight):
        return columns(weight, f_part).reshape(-1, f_part // tile, tile)

    gate_up_shard = jnp.concatenate([tiles(gate_weight), tiles(up_weight)], axis=2)
    owned, cot_rows, head_shard, gate_up_shard, down_shard = lax.optimization_barrier(
        (
            owned,
            mixed_cotangent[inverse],
            head_shard,
            gate_up_shard.reshape(-1, 2 * f_part),
            columns(down_weight, f_part),
        )
    )
    head_own = gather(head_shard)
    qkv_own, wo_own = head_own[:, :h_part], head_own[:, h_part:]
    gate_up_own = gather(gate_up_shard)
    down_own = gather(down_shard)
    cot_owned = exchange(cot_rows)

    lengths_row = lengths[0]
    token_spots = jnp.arange(group_rows, dtype=jnp.int32)
    seq_ends = jnp.cumsum(lengths_row)
    passed = token_spots[:, None] >= seq_ends[None, :]
    starts = jnp.sum(jnp.where(passed, lengths_row[None, :], 0), axis=1).astype(jnp.int32)
    places = (token_spots - starts).astype(F32)
    freqs = jnp.exp(jnp.arange(HALF, dtype=F32) * (-2.0 * math.log(THETA) / HEAD_SIZE))
    angles = freqs[:, None] * places[None, :]
    cosine, sine = jnp.cos(angles), jnp.sin(angles)
    low = starts[::block] // block
    start_row = starts[None, :]
    head_gains = jnp.stack([query_gain, key_gain]).astype(F32)[:, :, None]
    place = jnp.bitwise_xor(seq_index, jnp.arange(ranks, dtype=jnp.int32)).astype(jnp.int32)

    tok_f32 = owned.astype(F32)
    scale_one, normed_own = rms_parts(tok_f32, attn_full)
    normed = gather_chunks(normed_own, ranks)
    (last, first_place), (other, other_place) = normed[-1]
    alike = last is other
    last, other, cot_sent = lax.optimization_barrier((last, other[:8] if alike else other, cot_owned))
    normed[-1] = (last, first_place), (last if alike else other, other_place)
    cot = gather_start(cot_sent, ranks)
    qkv_raw = jnp.stack([dot(qkv_own, joined(pair), 0, 1) for pair in normed])
    attended, query, key, value, lse_table = attend(
        qkv_raw, low, place, start_row, cosine, sine, head_gains, ranks, local, block
    )
    attended, cot, wo_own = lax.optimization_barrier((attended, cot, wo_own))
    branch_sum, *_ = scatter_chunks(
        lambda k, given: dot(given[k], wo_own, 0, 1).astype(BF16), attended, ranks
    )
    resid = tok_f32 + branch_sum

    scale_two, normed_two_own = rms_parts(resid, ffn_full)
    chunks = gather_start(normed_two_own, ranks)
    results = up_chunk(0, gather_finish(chunks[:1], 1)[0], gate_up_own, None, ranks, tile, token_rows)
    chunks[1:], results, cot = lax.optimization_barrier((chunks[1:], results, cot))
    chunks = gather_finish(chunks, ranks)
    cot = cot + [m for m, _ in gather_finish(cot, ranks)[len(cot) :][0]] if ranks == 4 else cot
    for k in range(1, ranks):
        results = up_chunk(k, chunks[k], gate_up_own, results, ranks, tile, token_rows)
    factors, hidden, normed_two = results
    def scatter(terms):
        return lax.psum_scatter(
            terms.astype(BF16), "fsdp", scatter_dimension=0, tiled=True
        )

    def terms_of(left, right):
        return dot(left, right, 0, 0).astype(BF16)

    def down_part(k, hidden):
        return rows_times(hidden, k, down_own, token_rows)

    if ranks == 4:
        half = token_rows // 2
        corner = down_part(3, hidden)
        for_second, for_first = hop(corner[:half], 1, ranks), hop(corner[half:], 2, ranks)
        cot, hidden = lax.optimization_barrier((cot, hidden))
        cot = jnp.concatenate(cot)
        first, second = down_part(1, hidden), down_part(2, hidden)
        down_terms = terms_of(cot, hidden)
        for_first, for_second, down_terms, first, second = lax.optimization_barrier(
            (for_first, for_second, down_terms, first, second)
        )
        down_parts = [
            jnp.concatenate([first[:half], add(first[half:], for_first)]),
            jnp.concatenate([add(second[:half], for_second), second[half:]]),
        ]
    else:
        cot = jnp.concatenate(cot)
        down_parts = [down_part(k, hidden) for k in range(1, ranks)]
        down_terms = terms_of(cot, hidden)
    down_grad = scatter(down_terms)
    factors, down_parts, cot = lax.optimization_barrier((factors, down_parts, cot))
    down_sent = [hop(part, k + 1, ranks) for k, part in enumerate(down_parts)]
    gate_up_grad = hidden_back(cot, down_own, factors, tile)
    normed_two_grad, down_sent, down_out, _ = scatter_chunks(
        lambda k, given: rows_times(given, k, gate_up_own, token_rows),
        gate_up_grad,
        ranks,
        early=(down_sent, lambda a: a),
        late=(hidden, lambda a: down_part(0, a)),
    )
    resid_part, ffn_gain_part = rms_back(resid, scale_two, ffn_full, normed_two_grad)
    resid_grad = cot_owned.astype(F32) + resid_part
    branch_own = resid_grad.astype(BF16)
    branch_own, normed_two = lax.optimization_barrier((branch_own, normed_two))
    branch = gather_start(branch_own, ranks)
    gate_up_terms = terms_of(normed_two, gate_up_grad)
    down_out = sum((part.astype(F32) for part in down_sent), down_out.astype(F32))
    mixed_own = (resid + down_out).astype(BF16)

    def heads_of(rows):
        return dot(wo_own, rows, 0, 1).astype(BF16)

    attended_grad = [heads_of(rows) for rows in branch]
    branch, gate_up_terms = lax.optimization_barrier((branch, gate_up_terms))
    gate_up_out = scatter(gate_up_terms)
    branch = gather_finish(branch, ranks)
    if ranks == 4:
        attended_grad.append(heads_of(joined(branch[-1])))
    attended_grad = jnp.stack(attended_grad)
    down_all = gather_start(down_grad, ranks)
    d_heads, head_gain_parts = attend_back(
        qkv_raw, low, place, start_row, cosine, sine, head_gains, query, key, value, lse_table,
        attended, attended_grad, ranks, local, block,
    )
    d_heads, down_all, back_mixed = lax.optimization_barrier(
        (d_heads, down_all, exchange(mixed_own))
    )

    normed_grad, _, head_terms, _ = scatter_chunks(
        lambda k, given: dot(given[k], qkv_own, 0, 1).astype(BF16),
        d_heads,
        ranks,
        late=(
            (d_heads, attended),
            lambda a: head_outer(a[0], normed, a[1], branch),
        ),
    )
    tok_part, attn_gain_part = rms_back(tok_f32, scale_one, attn_full, normed_grad)
    input_grad_own = (resid_grad + tok_part).astype(BF16)
    packed = jnp.concatenate(
        [
            attn_gain_part.reshape(groups, -1),
            ffn_gain_part.reshape(groups, -1),
            jnp.broadcast_to(head_gain_parts[0, :, 0], (groups, HEAD_SIZE)),
            jnp.broadcast_to(head_gain_parts[1, :, 0], (groups, HEAD_SIZE)),
        ],
        axis=1,
    )
    input_grad_own, packed, back_mixed, down_all = lax.optimization_barrier(
        (input_grad_own, packed, back_mixed, down_all)
    )
    back_grad = exchange(input_grad_own)
    packed, back_grad = lax.optimization_barrier((packed, back_grad))
    head_terms, gate_up_out = lax.optimization_barrier((head_terms, gate_up_out))
    head_grad = scatter(head_terms)

    down_all = gather_finish(down_all, ranks)
    gate_up_all = gather_chunks(gate_up_out, ranks)
    head_all = gather_chunks(head_grad, ranks)

    summed = jnp.sum(exchange(packed), axis=0)
    summed = summed.reshape(8, -1)
    for bit in range(ranks.bit_length() - 1):
        summed = summed + hop(summed, 1 << bit, ranks)
    summed = summed.reshape(-1)

    def of_heads(start, width):
        return widen([head_all], place, [(0, width)], width, start // width, ranks, shard)

    def of_tiles(side):
        spans = [
            (at + side * tile, at + (side + 1) * tile) for at in range(0, 2 * f_part, 2 * tile)
        ]
        return widen([gate_up_all], place, spans, 2 * f_part, 0, ranks, shard)

    return (
        back_mixed[send_spot],
        back_grad[send_spot],
        of_heads(0, q_part),
        of_heads(q_part, k_part),
        of_heads(q_part + k_part, k_part),
        widen([head_all], place, [(h_part, h_part + q_part)], h_part + q_part, 0, ranks, shard),
        of_tiles(0),
        of_tiles(1),
        widen([down_all], place, [(0, f_part)], f_part, 0, ranks, shard),
        summed[:gain_rows],
        summed[gain_rows : 2 * gain_rows],
        summed[2 * gain_rows : 2 * gain_rows + HEAD_SIZE],
        summed[2 * gain_rows + HEAD_SIZE :],
    )


def solution(mesh):
    rows = P("fsdp", None)
    tokens = P(("fsdp", "seq"), None)
    in_specs = (
        tokens, tokens, rows, P(("fsdp", "seq")), rows, rows, rows, rows, rows, rows, rows,
        P("fsdp"), P("fsdp"), P(), P(),
    )
    out_specs = (
        tokens, tokens, rows, rows, rows, rows, rows, rows, rows,
        P("fsdp"), P("fsdp"), P(), P(),
    )
    return jax.shard_map(body, mesh=mesh, in_specs=in_specs, out_specs=out_specs, check_vma=False)
```

```python
import functools
import math

import jax
import jax.numpy as jnp
from jax import lax
from jax.experimental import pallas as pl
from jax.experimental.pallas import tpu as pltpu
from jax.sharding import PartitionSpec as P

QUERY_HEADS = 32
KEY_VALUE_HEADS = 8
HEAD_SIZE = 64
HALF = HEAD_SIZE // 2
GROUP_HEADS = QUERY_HEADS // KEY_VALUE_HEADS

EPS = 1e-05
THETA = 1000000.0
SCALE = 1.0 / math.sqrt(HEAD_SIZE)
LOG2E = math.log2(math.e)
F32 = jnp.float32
BF16 = jnp.bfloat16


def dot(left, right, left_dim, right_dim):
    return lax.dot_general(
        left, right, (((left_dim,), (right_dim,)), ((), ())), preferred_element_type=F32
    )


def rms_rope(raw, gain, cosine, sine):
    normed = raw * lax.rsqrt(jnp.mean(raw * raw, axis=0, keepdims=True) + EPS) * gain
    first, second = normed[:HALF], normed[HALF:]
    return jnp.concatenate(
        [first * cosine - second * sine, second * cosine + first * sine], axis=0
    )


def rms_rope_back(raw, gain, cosine, sine, grad):
    first, second = grad[:HALF], grad[HALF:]
    turned = jnp.concatenate(
        [first * cosine + second * sine, second * cosine - first * sine], axis=0
    )
    scale = lax.rsqrt(jnp.mean(raw * raw, axis=0, keepdims=True) + EPS)
    unit = raw * scale
    weighted = gain * turned
    raw_grad = scale * (weighted - unit * jnp.mean(weighted * unit, axis=0, keepdims=True))
    return raw_grad, turned * unit


def attend_kernel(
    block, low_ref, order_ref, q_raw, k_raw, v_raw, start_ref, cos_ref, sin_ref, gains_ref,
    out_ref, q_out, k_out, v_out, lse_ref, k_rows, acc, total,
):
    step = pl.program_id(1)
    query_gain, key_gain = gains_ref[0], gains_ref[1]

    @pl.when(step == 0)
    def _():
        token_rows = k_raw.shape[2]
        for r in range(k_raw.shape[0]):
            part = slice(r * token_rows, (r + 1) * token_rows)
            at = order_ref[r]
            key = rms_rope(k_raw[at], key_gain, cos_ref[:, part], sin_ref[:, part])
            k_out[:, part] = key.astype(BF16)
            k_rows[part, :] = key.T.astype(BF16)
            v_out[:, part] = v_raw[at].astype(BF16)

    columns = pl.ds(pl.multiple_of(step * block, block), block)
    cosine, sine = cos_ref[:, columns], sin_ref[:, columns]
    for g in range(GROUP_HEADS):
        rows = slice(g * HEAD_SIZE, (g + 1) * HEAD_SIZE)
        q_out[rows, :] = rms_rope(q_raw[0, rows, :], query_gain, cosine, sine).astype(BF16)
    acc[...] = jnp.zeros_like(acc)
    total[...] = jnp.zeros_like(total)
    starts = start_ref[...]
    spots = step * block + lax.broadcasted_iota(jnp.int32, (1, block), 1)

    def inner(j, carry):
        keys = pl.ds(pl.multiple_of(j * block, block), block)
        key_rows = k_rows[keys, :]
        value = v_out[:, keys]
        key_spots = j * block + lax.broadcasted_iota(jnp.int32, (block, 1), 0)
        allowed = (key_spots >= starts) & (key_spots <= spots)
        for g in range(GROUP_HEADS):
            rows = slice(g * HEAD_SIZE, (g + 1) * HEAD_SIZE)
            score = dot(key_rows, q_out[rows, :], 1, 0)
            prob = jnp.where(allowed, jnp.exp2(score * (SCALE * LOG2E)), 0.0)
            total[g : g + 1, :] += jnp.sum(prob, axis=0, keepdims=True)
            acc[rows, :] += dot(value, prob.astype(BF16), 1, 0)
        return carry

    lax.fori_loop(low_ref[step], step + 1, inner, 0)
    for g in range(GROUP_HEADS):
        rows = slice(g * HEAD_SIZE, (g + 1) * HEAD_SIZE)
        summed = total[g : g + 1, :]
        out_ref[0, rows, :] = (acc[rows, :] / summed).astype(BF16)
        lse_ref[0, g : g + 1, :] = jnp.log2(summed)


def attend_back_kernel(
    block, spans, low_ref, order_ref, q_raw, k_raw, start_ref, cos_ref, sin_ref, gains_ref,
    q_ref, k_ref, v_ref, lse_ref, out_ref, grad_ref,
    d_ref, gain_out, k_rows, v_rows, dq, dk, dv, gain_acc,
):
    head, step = pl.program_id(0), pl.program_id(1)
    steps = pl.num_programs(1)
    local = pl.num_programs(0)
    query_gain, key_gain = gains_ref[0], gains_ref[1]
    width = GROUP_HEADS * HEAD_SIZE
    token_rows = spans * block

    @pl.when((head == 0) & (step == 0))
    def _():
        gain_acc[...] = jnp.zeros_like(gain_acc)
        gain_out[...] = jnp.zeros_like(gain_out)

    @pl.when(step == 0)
    def _():
        k_rows[...] = k_ref[...].astype(F32).T.astype(BF16)
        v_rows[...] = v_ref[...].astype(F32).T.astype(BF16)
        dk[...] = jnp.zeros_like(dk)
        dv[...] = jnp.zeros_like(dv)

    columns = pl.ds(pl.multiple_of(step * block, block), block)
    cosine, sine = cos_ref[:, columns], sin_ref[:, columns]
    dq[...] = jnp.zeros_like(dq)
    starts = start_ref[...]
    spots = step * block + lax.broadcasted_iota(jnp.int32, (1, block), 1)
    inner_sums = [
        jnp.sum(
            out_ref[0, g * HEAD_SIZE : (g + 1) * HEAD_SIZE, :].astype(F32)
            * grad_ref[0, g * HEAD_SIZE : (g + 1) * HEAD_SIZE, :].astype(F32),
            axis=0,
            keepdims=True,
        )
        for g in range(GROUP_HEADS)
    ]

    def inner(j, carry):
        keys = pl.ds(pl.multiple_of(j * block, block), block)
        key_rows, value_rows, key = k_rows[keys, :], v_rows[keys, :], k_ref[:, keys]
        key_spots = j * block + lax.broadcasted_iota(jnp.int32, (block, 1), 0)
        allowed = (key_spots >= starts) & (key_spots <= spots)
        key_sum = jnp.zeros((HEAD_SIZE, block), F32)
        value_sum = jnp.zeros((HEAD_SIZE, block), F32)
        for g in range(GROUP_HEADS):
            rows = slice(g * HEAD_SIZE, (g + 1) * HEAD_SIZE)
            query, grad = q_ref[rows, :], grad_ref[0, rows, :]
            score = dot(key_rows, query, 1, 0) * (SCALE * LOG2E) - lse_ref[0, g : g + 1, :]
            prob = jnp.where(allowed, jnp.exp2(score), 0.0)
            prob_grad = dot(value_rows, grad, 1, 0)
            score_grad = (prob * (prob_grad - inner_sums[g])).astype(BF16)
            value_sum += dot(grad, prob.astype(BF16), 1, 1)
            key_sum += dot(query, score_grad, 1, 1)
            dq[rows, :] += dot(key, score_grad, 1, 0)
        dk[:, keys] += key_sum
        dv[:, keys] += value_sum
        return carry

    lax.fori_loop(low_ref[step], step + 1, inner, 0)
    span = step // spans
    inside = pl.ds(pl.multiple_of((step % spans) * block, block), block)
    for g in range(GROUP_HEADS):
        rows = slice(g * HEAD_SIZE, (g + 1) * HEAD_SIZE)
        grad = (dq[rows, :] * SCALE).astype(BF16).astype(F32)
        raw_grad, terms = rms_rope_back(q_raw[0, rows, :], query_gain, cosine, sine, grad)
        d_ref[order_ref[span], pl.ds(pl.multiple_of(head * width + g * HEAD_SIZE, HEAD_SIZE), HEAD_SIZE), inside] = (
            raw_grad.astype(BF16)
        )
        gain_acc[...] += terms

    @pl.when(step == steps - 1)
    def _():
        key_at = pl.ds(pl.multiple_of(local * width + head * HEAD_SIZE, HEAD_SIZE), HEAD_SIZE)
        value_at = pl.ds(
            pl.multiple_of(local * (width + HEAD_SIZE) + head * HEAD_SIZE, HEAD_SIZE), HEAD_SIZE
        )
        for r in range(d_ref.shape[0]):
            part = slice(r * token_rows, (r + 1) * token_rows)
            grad = (dk[:, part] * SCALE).astype(BF16).astype(F32)
            raw_grad, terms = rms_rope_back(
                k_raw[order_ref[r]], key_gain, cos_ref[:, part], sin_ref[:, part], grad
            )
            d_ref[order_ref[r], key_at, :] = raw_grad.astype(BF16)
            d_ref[order_ref[r], value_at, :] = dv[:, part].astype(BF16)
            gain_out[1] += jnp.broadcast_to(
                jnp.sum(terms, axis=1, keepdims=True), gain_out.shape[1:]
            )

    @pl.when((step == steps - 1) & (head == local - 1))
    def _():
        gain_out[0] = jnp.broadcast_to(
            jnp.sum(gain_acc[...], axis=1, keepdims=True), gain_out.shape[1:]
        )


def attention_specs(block, group_rows, local, spans):
    width = GROUP_HEADS * HEAD_SIZE
    tables = [
        pl.BlockSpec((1, block), lambda h, s, low, order: (0, s)),
        pl.BlockSpec((HALF, group_rows), lambda h, s, low, order: (0, 0)),
        pl.BlockSpec((HALF, group_rows), lambda h, s, low, order: (0, 0)),
        pl.BlockSpec((2, HEAD_SIZE, 1), lambda h, s, low, order: (0, 0, 0)),
    ]
    q_block = pl.BlockSpec((width, block), lambda h, s, low, order: (h, s))
    k_block = pl.BlockSpec((HEAD_SIZE, group_rows), lambda h, s, low, order: (h, 0))
    raw_q = pl.BlockSpec(
        (1, width, block), lambda h, s, low, order: (order[s // spans], h, s % spans)
    )
    ranks, token_rows = group_rows // (spans * block), spans * block
    raw_k = pl.BlockSpec(
        (ranks, HEAD_SIZE, token_rows),
        lambda h, s, low, order: (0, local * GROUP_HEADS + h, 0),
    )
    raw_v = pl.BlockSpec(
        (ranks, HEAD_SIZE, token_rows),
        lambda h, s, low, order: (0, local * (GROUP_HEADS + 1) + h, 0),
    )
    lse = pl.BlockSpec((1, 8, block), lambda h, s, low, order: (h, 0, s))
    return tables, q_block, k_block, raw_q, raw_k, raw_v, lse


def attend(qkv_raw, low, order, starts, cosine, sine, gains, ranks, local, block):
    token_rows = qkv_raw.shape[2]
    group_rows = token_rows * ranks
    spans = token_rows // block
    width = GROUP_HEADS * HEAD_SIZE
    tables, q_block, k_block, raw_q, raw_k, raw_v, lse = attention_specs(
        block, group_rows, local, spans
    )
    return pl.pallas_call(
        functools.partial(attend_kernel, block),
        out_shape=(
            jax.ShapeDtypeStruct((ranks, local * width, token_rows), BF16),
            jax.ShapeDtypeStruct((local * width, group_rows), BF16),
            jax.ShapeDtypeStruct((local * HEAD_SIZE, group_rows), BF16),
            jax.ShapeDtypeStruct((local * HEAD_SIZE, group_rows), BF16),
            jax.ShapeDtypeStruct((local, 8, group_rows), F32),
        ),
        grid_spec=pltpu.PrefetchScalarGridSpec(
            num_scalar_prefetch=2,
            grid=(local, group_rows // block),
            in_specs=[raw_q, raw_k, raw_v, *tables],
            out_specs=[raw_q, q_block, k_block, k_block, lse],
            scratch_shapes=[
                pltpu.VMEM((group_rows, HEAD_SIZE), BF16),
                pltpu.VMEM((width, block), F32),
                pltpu.VMEM((8, block), F32),
            ],
        ),
        compiler_params=pltpu.CompilerParams(vmem_limit_bytes=40 << 20),
        cost_estimate=pl.CostEstimate(flops=1 << 20, bytes_accessed=1 << 20, transcendentals=0),
        name="attend",
    )(low, order, qkv_raw, qkv_raw, qkv_raw, starts, cosine, sine, gains)


def attend_back(
    qkv_raw, low, order, starts, cosine, sine, gains, query, key, value, lse_table, attended, grad,
    ranks, local, block,
):
    token_rows = qkv_raw.shape[2]
    group_rows = token_rows * ranks
    spans = token_rows // block
    width = GROUP_HEADS * HEAD_SIZE
    total = local * (width + 2 * HEAD_SIZE)
    tables, q_block, k_block, raw_q, raw_k, _, lse = attention_specs(
        block, group_rows, local, spans
    )
    return pl.pallas_call(
        functools.partial(attend_back_kernel, block, spans),
        out_shape=(
            jax.ShapeDtypeStruct((ranks, total, token_rows), BF16),
            jax.ShapeDtypeStruct((2, HEAD_SIZE, 128), F32),
        ),
        grid_spec=pltpu.PrefetchScalarGridSpec(
            num_scalar_prefetch=2,
            grid=(local, group_rows // block),
            in_specs=[
                raw_q, raw_k, *tables, q_block, k_block, k_block, lse, raw_q, raw_q,
            ],
            out_specs=[
                pl.BlockSpec((ranks, total, token_rows), lambda h, s, low, order: (0, 0, 0)),
                pl.BlockSpec((2, HEAD_SIZE, 128), lambda h, s, low, order: (0, 0, 0)),
            ],
            scratch_shapes=[
                pltpu.VMEM((group_rows, HEAD_SIZE), BF16),
                pltpu.VMEM((group_rows, HEAD_SIZE), BF16),
                pltpu.VMEM((width, block), F32),
                pltpu.VMEM((HEAD_SIZE, group_rows), F32),
                pltpu.VMEM((HEAD_SIZE, group_rows), F32),
                pltpu.VMEM((HEAD_SIZE, block), F32),
            ],
        ),
        compiler_params=pltpu.CompilerParams(vmem_limit_bytes=48 << 20),
        cost_estimate=pl.CostEstimate(
            flops=400 * 10**9, bytes_accessed=1 << 20, transcendentals=0
        ),
        name="attend_back",
    )(
        low, order, qkv_raw, qkv_raw, starts, cosine, sine, gains, query, key, value, lse_table,
        attended, grad,
    )


def rms_parts(rows, gain):
    scale = lax.rsqrt(jnp.mean(rows * rows, axis=-1, keepdims=True) + EPS)
    return scale, (rows * scale * gain).astype(BF16)


def rms_back(rows, scale, gain, grad):
    unit = rows * scale
    weighted = grad * gain
    row_grad = scale * (weighted - unit * jnp.mean(weighted * unit, axis=-1, keepdims=True))
    return row_grad, jnp.sum(grad * unit, axis=0)


def hop(rows, distance, ranks):
    return lax.ppermute(rows, "seq", [(i, i ^ distance) for i in range(ranks)])


def after(values, *first):
    return lax.optimization_barrier((values, first))[0]


def gather_start(rows, ranks):
    return [rows] + [hop(rows, k, ranks) for k in range(1, ranks if ranks != 4 else 3)]


def gather_finish(chunks, ranks):
    half = chunks[0].shape[0] // 2
    pairs = [((m, 0), (m, 1)) for m in chunks]
    if ranks == 4:
        corner = hop(chunks[1][:half], 2, ranks), hop(chunks[2][half:], 1, ranks)
        pairs.append(((corner[0], 0), (corner[1], 0)))
    return pairs


def gather_chunks(rows, ranks):
    return gather_finish(gather_start(rows, ranks), ranks)


def joined(pair):
    (first, _), (second, _) = pair
    return first if first is second else jnp.concatenate([first, second])


def pieces_of(pairs):
    flat = [piece for pair in pairs for piece in pair]
    return [m for m, _ in flat], [at for _, at in flat]


def add(a, b):
    return (a.astype(F32) + b.astype(F32)).astype(BF16)


def scatter_chunks(make, given, ranks, early=((), None), late=((), None), keep=False, wait=()):
    def run(work, arrays):
        return work[1](arrays) if work[1] else ()

    if ranks != 4:
        sent = [make(k, given) for k in range(1, ranks)]
        sent, first, second = lax.optimization_barrier((sent, early[0], late[0]))
        own = make(0, given)
        more = run(early, first), run(late, second)
        moved = [hop(part, k + 1, ranks) for k, part in enumerate(sent)]
        moved, own, wait = lax.optimization_barrier((moved, own, wait))
        return sum((m.astype(F32) for m in moved), own.astype(F32)), *more, wait
    corner = make(3, given)
    half = corner.shape[0] // 2
    corner, given, arrays = lax.optimization_barrier((corner, given, early[0]))
    for_second = hop(corner[:half], 1, ranks)
    for_first = hop(corner[half:], 2, ranks)
    first = make(1, given)
    top = first[:half]
    top, given = lax.optimization_barrier((top, given))
    top = hop(top, 1, ranks)
    second, early = make(2, given), run(early, arrays)

    bottom = second[half:]
    first, second = add(first[half:], for_first), add(second[:half], for_second)
    bottom, first, second, given, early, arrays = lax.optimization_barrier(
        (bottom, first, second, given, early, late[0])
    )
    own, late = make(0, given), run(late, arrays)
    moved = top, hop(first, 1, ranks), hop(second, 2, ranks), hop(bottom, 2, ranks), own
    if keep:
        moved, wait = lax.optimization_barrier((moved, wait))
    else:
        moved, late, wait = lax.optimization_barrier((moved, late, wait))
    top, first, second, bottom, own = moved
    first = jnp.concatenate([top, first]).astype(F32)
    second = jnp.concatenate([second, bottom]).astype(F32)
    return own.astype(F32) + first + second, early, late, wait


def rows_kernel(left, right, out):
    out[...] = dot(left[...], right[...], 1, 1).astype(BF16)


def rows_times(left, k, right, rows):
    width, depth = right.shape
    tile = min(512, width)
    return pl.pallas_call(
        rows_kernel,
        out_shape=jax.ShapeDtypeStruct((rows, width), BF16),
        grid=(width // tile,),
        in_specs=[
            pl.BlockSpec((rows, depth), lambda t: (k, 0)),
            pl.BlockSpec((tile, depth), lambda t: (t, 0)),
        ],
        out_specs=pl.BlockSpec((rows, tile), lambda t: (0, t)),
        compiler_params=pltpu.CompilerParams(vmem_limit_bytes=48 << 20),
        cost_estimate=pl.CostEstimate(flops=1 << 20, bytes_accessed=1 << 20, transcendentals=0),
        name="rows_times",
    )(left, right)


def up_kernel(tile, xa, xb, w_ref, *rest):
    f_ref, hid_ref, x_ref, x_all = rest[-4:]
    half = xa.shape[0]

    @pl.when(pl.program_id(0) == 0)
    def _():
        x_all[:half, :] = xa[...]
        x_all[half:, :] = xb[...]
        x_ref[...] = x_all[...]

    for i in range(w_ref.shape[1] // (2 * tile)):
        left, right = 2 * i * tile, (2 * i + 1) * tile
        both = dot(x_all[...], w_ref[:, left : left + 2 * tile], 1, 0)
        gate, up = both[:, :tile], both[:, tile:]
        gated = jax.nn.sigmoid(gate)
        silu = gate * gated
        hid_ref[:, i * tile : (i + 1) * tile] = (silu * up).astype(BF16)
        f_ref[:, left:right] = (up * (gated + silu * (1.0 - gated))).astype(BF16)
        f_ref[:, right : right + tile] = silu.astype(BF16)


def up_chunk(k, x, gate_up, before, ranks, tile, rows):
    arrays, places = pieces_of([x])
    half, features = rows // 2, arrays[0].shape[1]
    width = gate_up.shape[1]
    halves = [pl.BlockSpec((half, features), lambda t, at=at: (at, 0)) for at in places]
    step = min(2 * tile, width // 2)
    kept = [] if before is None else list(before)
    return pl.pallas_call(
        functools.partial(up_kernel, tile),
        out_shape=(
            jax.ShapeDtypeStruct((ranks * rows, width), BF16),
            jax.ShapeDtypeStruct((ranks * rows, width // 2), BF16),
            jax.ShapeDtypeStruct((ranks * rows, features), BF16),
        ),
        grid=(width // (2 * step),),
        in_specs=halves
        + [pl.BlockSpec((features, 2 * step), lambda t: (0, t))]
        + [pl.BlockSpec(memory_space=pl.ANY)] * len(kept),
        out_specs=(
            pl.BlockSpec((rows, 2 * step), lambda t: (k, t)),
            pl.BlockSpec((rows, step), lambda t: (k, t)),
            pl.BlockSpec((rows, features), lambda t: (k, 0)),
        ),
        scratch_shapes=[pltpu.VMEM((rows, features), BF16)],
        input_output_aliases={3 + i: i for i in range(len(kept))},
        compiler_params=pltpu.CompilerParams(vmem_limit_bytes=48 << 20),
        cost_estimate=pl.CostEstimate(flops=1 << 20, bytes_accessed=1 << 20, transcendentals=0),
        name="up_chunk",
    )(*arrays, gate_up, *kept)


def head_outer_kernel(count, d_ref, a_ref, *refs):
    out = refs[-1]
    at = 0
    for left, pieces in ((d_ref, refs[:count]), (a_ref, refs[count : 2 * count])):
        half = pieces[0].shape[0]
        total = sum(
            dot(left[i // 2, :, (i % 2) * half : (i % 2 + 1) * half], piece[...], 1, 0)
            for i, piece in enumerate(pieces)
        )
        out[:, at : at + left.shape[1]] = total.T.astype(BF16)
        at += left.shape[1]


def head_outer(d_heads, normed, attended, branch):
    ranks, width, rows = d_heads.shape
    more = attended.shape[1]
    left, left_places = pieces_of(normed)
    right, right_places = pieces_of(branch)
    features = left[0].shape[1]
    tile = min(512, features)

    def heads(w):
        return pl.BlockSpec((ranks, w, rows), lambda t: (0, 0, 0))

    tokens = [
        pl.BlockSpec((rows // 2, tile), lambda t, at=at: (at, t))
        for at in left_places + right_places
    ]
    return pl.pallas_call(
        functools.partial(head_outer_kernel, len(left)),
        out_shape=jax.ShapeDtypeStruct((features, width + more), BF16),
        grid=(features // tile,),
        in_specs=[heads(width), heads(more), *tokens],
        out_specs=pl.BlockSpec((tile, width + more), lambda t: (t, 0)),
        compiler_params=pltpu.CompilerParams(vmem_limit_bytes=48 << 20),
        cost_estimate=pl.CostEstimate(flops=1 << 20, bytes_accessed=1 << 20, transcendentals=0),
        name="head_outer",
    )(d_heads, attended, *left, *right)


def hidden_back_kernel(tile, c_ref, w_ref, f_ref, d_ref):
    rows = c_ref.shape[0] // 4
    for r in range(4):
        at = slice(r * rows, (r + 1) * rows)
        hidden_grad = dot(c_ref[at, :], w_ref[...], 1, 0)
        for i in range(w_ref.shape[1] // tile):
            left, right = 2 * i * tile, (2 * i + 1) * tile
            part = hidden_grad[:, i * tile : (i + 1) * tile]
            d_ref[at, left:right] = (part * f_ref[at, left:right].astype(F32)).astype(BF16)
            d_ref[at, right : right + tile] = (
                part * f_ref[at, right : right + tile].astype(F32)
            ).astype(BF16)


def hidden_back(cot, down, factors, tile):
    group_rows, features = cot.shape
    width = down.shape[1]
    step = min(2 * tile, width)
    return pl.pallas_call(
        functools.partial(hidden_back_kernel, tile),
        out_shape=jax.ShapeDtypeStruct((group_rows, 2 * width), BF16),
        grid=(width // step,),
        in_specs=[
            pl.BlockSpec((group_rows, features), lambda t: (0, 0)),
            pl.BlockSpec((features, step), lambda t: (0, t)),
            pl.BlockSpec((group_rows, 2 * step), lambda t: (0, t)),
        ],
        out_specs=pl.BlockSpec((group_rows, 2 * step), lambda t: (0, t)),
        compiler_params=pltpu.CompilerParams(vmem_limit_bytes=56 << 20),
        cost_estimate=pl.CostEstimate(flops=1 << 20, bytes_accessed=1 << 20, transcendentals=0),
        name="hidden_back",
    )(cot, down, factors)


def widen(pieces, place, columns, part, total, ranks, rows):
    each = sum(stop - start for start, stop in columns)
    width = each * len(pieces)
    if ranks != 4:

        def picked(chunk):
            return jnp.concatenate([chunk[:, a:b] for a, b in columns], axis=1)

        stacked = jnp.stack(
            [
                jnp.concatenate(
                    [picked(joined(group[k])) for group in pieces], axis=1
                )
                for k in range(ranks)
            ]
        )
        ordered = jnp.swapaxes(jnp.take(stacked, place, axis=0), 0, 1)
        return ordered.reshape(rows, ranks * width).astype(F32)
    half = rows // 2
    flat, places = pieces_of([pair for group in pieces for pair in group])
    counts = len(pieces)
    whole = [
        pl.BlockSpec((half, part), lambda k, place, at=at: (at, total)) for at in places
    ]

    def kernel(place_ref, *refs):
        out = refs[-1]
        for k in range(ranks):

            @pl.when(pl.program_id(0) == k)
            def _(k=k):
                at = 0
                for group in range(counts):
                    for start, stop in columns:
                        for side in range(2):
                            source = refs[(group * ranks + k) * 2 + side]
                            out[side * half : (side + 1) * half, at : at + stop - start] = source[
                                :, start:stop
                            ].astype(F32)
                        at += stop - start

    return pl.pallas_call(
        kernel,
        out_shape=jax.ShapeDtypeStruct((rows, ranks * width), F32),
        grid_spec=pltpu.PrefetchScalarGridSpec(
            num_scalar_prefetch=1,
            grid=(ranks,),
            in_specs=whole,
            out_specs=pl.BlockSpec((rows, width), lambda k, place: (0, place[k])),
        ),
        compiler_params=pltpu.CompilerParams(vmem_limit_bytes=48 << 20),
        cost_estimate=pl.CostEstimate(
            flops=rows * width * ranks * 15000, bytes_accessed=1 << 20, transcendentals=0
        ),
        name="widen",
    )(place, *flat)


def body(
    tokens, mixed_cotangent, lengths, owner_slot, q_weight, key_projection, value_projection,
    out_weight, gate_weight, up_weight, down_weight, attn_gain, ffn_gain, query_gain, key_gain,
):
    groups = lax.axis_size("fsdp")
    ranks = lax.axis_size("seq")
    seq_index = lax.axis_index("seq")
    token_rows, features = tokens.shape
    slice_rows = token_rows // groups
    group_rows = token_rows * ranks
    local = KEY_VALUE_HEADS // ranks
    q_part = q_weight.shape[1] // ranks
    k_part = key_projection.shape[1] // ranks
    f_part = gate_weight.shape[1] // ranks
    h_part = q_part + 2 * k_part
    block = min(256, token_rows)
    tile = min(256, f_part)
    gain_rows = attn_gain.shape[0]
    shard = q_weight.shape[0]

    local_slot = owner_slot % token_rows
    target = owner_slot // token_rows // ranks
    send_spot = target * slice_rows + local_slot % slice_rows
    inverse = (
        jnp.zeros((token_rows,), jnp.int32)
        .at[send_spot]
        .set(jnp.arange(token_rows, dtype=jnp.int32))
    )

    def exchange(rows):
        return lax.all_to_all(rows, "fsdp", split_axis=0, concat_axis=0, tiled=True)

    both_gains = jnp.concatenate([attn_gain, ffn_gain])
    gains_full = exchange(jnp.broadcast_to(both_gains, (groups, 2 * gain_rows))).astype(F32)
    token_rows_sent, gains_full = lax.optimization_barrier((tokens[inverse], gains_full))
    owned = exchange(token_rows_sent)
    attn_full = gains_full[:, :gain_rows].reshape(features)
    ffn_full = gains_full[:, gain_rows:].reshape(features)

    def columns(weight, width):
        return lax.dynamic_slice_in_dim(weight, seq_index * width, width, 1)

    def gather(weight):
        return lax.all_gather(weight, "fsdp", axis=0, tiled=True)

    head_shard = (
        jnp.concatenate(
            [
                columns(q_weight, q_part),
                columns(key_projection, k_part),
                columns(value_projection, k_part),
                columns(out_weight, q_part),
            ],
            axis=1,
        )
    )

    def tiles(weight):
        return columns(weight, f_part).reshape(-1, f_part // tile, tile)

    gate_up_shard = jnp.concatenate([tiles(gate_weight), tiles(up_weight)], axis=2)
    owned, cot_rows, head_shard, gate_up_shard, down_shard = lax.optimization_barrier(
        (
            owned,
            mixed_cotangent[inverse],
            head_shard,
            gate_up_shard.reshape(-1, 2 * f_part),
            columns(down_weight, f_part),
        )
    )
    head_own = gather(head_shard)
    qkv_own, wo_own = head_own[:, :h_part], head_own[:, h_part:]
    gate_up_own = gather(gate_up_shard)
    down_own = gather(down_shard)
    cot_owned = exchange(cot_rows)

    lengths_row = lengths[0]
    token_spots = jnp.arange(group_rows, dtype=jnp.int32)
    seq_ends = jnp.cumsum(lengths_row)
    passed = token_spots[:, None] >= seq_ends[None, :]
    starts = jnp.sum(jnp.where(passed, lengths_row[None, :], 0), axis=1).astype(jnp.int32)
    places = (token_spots - starts).astype(F32)
    freqs = jnp.exp(jnp.arange(HALF, dtype=F32) * (-2.0 * math.log(THETA) / HEAD_SIZE))
    angles = freqs[:, None] * places[None, :]
    cosine, sine = jnp.cos(angles), jnp.sin(angles)
    low = starts[::block] // block
    start_row = starts[None, :]
    head_gains = jnp.stack([query_gain, key_gain]).astype(F32)[:, :, None]
    place = jnp.bitwise_xor(seq_index, jnp.arange(ranks, dtype=jnp.int32)).astype(jnp.int32)

    tok_f32 = owned.astype(F32)
    scale_one, normed_own = rms_parts(tok_f32, attn_full)
    normed = gather_chunks(normed_own, ranks)
    (last, first_place), (other, other_place) = normed[-1]
    alike = last is other
    last, other, cot_sent = lax.optimization_barrier((last, other[:8] if alike else other, cot_owned))
    normed[-1] = (last, first_place), (last if alike else other, other_place)
    cot = gather_start(cot_sent, ranks)
    qkv_raw = jnp.stack([dot(qkv_own, joined(pair), 0, 1) for pair in normed])
    attended, query, key, value, lse_table = attend(
        qkv_raw, low, place, start_row, cosine, sine, head_gains, ranks, local, block
    )
    attended, cot, wo_own = lax.optimization_barrier((attended, cot, wo_own))
    branch_sum, *_ = scatter_chunks(
        lambda k, given: dot(given[k], wo_own, 0, 1).astype(BF16), attended, ranks
    )
    resid = tok_f32 + branch_sum

    scale_two, normed_two_own = rms_parts(resid, ffn_full)
    chunks = gather_start(normed_two_own, ranks)
    results = up_chunk(0, gather_finish(chunks[:1], 1)[0], gate_up_own, None, ranks, tile, token_rows)
    chunks[1:], results, cot = lax.optimization_barrier((chunks[1:], results, cot))
    chunks = gather_finish(chunks, ranks)
    cot = cot + [m for m, _ in gather_finish(cot, ranks)[len(cot) :][0]] if ranks == 4 else cot
    for k in range(1, ranks):
        results = up_chunk(k, chunks[k], gate_up_own, results, ranks, tile, token_rows)
    factors, hidden, normed_two = results
    def scatter(terms):
        return lax.psum_scatter(
            terms.astype(BF16), "fsdp", scatter_dimension=0, tiled=True
        )

    def terms_of(left, right):
        return dot(left, right, 0, 0).astype(BF16)

    def down_part(k, hidden):
        return rows_times(hidden, k, down_own, token_rows)

    if ranks == 4:
        half = token_rows // 2
        corner = down_part(3, hidden)
        for_second, for_first = hop(corner[:half], 1, ranks), hop(corner[half:], 2, ranks)
        cot, hidden = lax.optimization_barrier((cot, hidden))
        cot = jnp.concatenate(cot)
        first, second = down_part(1, hidden), down_part(2, hidden)
        down_terms = terms_of(cot, hidden)
        for_first, for_second, down_terms, first, second = lax.optimization_barrier(
            (for_first, for_second, down_terms, first, second)
        )
        down_parts = [
            jnp.concatenate([first[:half], add(first[half:], for_first)]),
            jnp.concatenate([add(second[:half], for_second), second[half:]]),
        ]
    else:
        cot = jnp.concatenate(cot)
        down_parts = [down_part(k, hidden) for k in range(1, ranks)]
        down_terms = terms_of(cot, hidden)
    down_grad = scatter(down_terms)
    factors, down_parts, cot = lax.optimization_barrier((factors, down_parts, cot))
    down_sent = [hop(part, k + 1, ranks) for k, part in enumerate(down_parts)]
    gate_up_grad = hidden_back(cot, down_own, factors, tile)
    normed_two_grad, (down_sent, left_terms), down_out, _ = scatter_chunks(
        lambda k, given: rows_times(given, k, gate_up_own, token_rows),
        gate_up_grad,
        ranks,
        early=(
            (down_sent, normed_two),
            lambda a: (a[0], terms_of(a[1], gate_up_grad[:, :f_part])),
        ),
        late=(hidden, lambda a: down_part(0, a)),
    )
    left_terms, down_grad = lax.optimization_barrier((left_terms, down_grad))
    left_out = scatter(left_terms)
    resid_part, ffn_gain_part = rms_back(resid, scale_two, ffn_full, normed_two_grad)
    resid_grad = cot_owned.astype(F32) + resid_part
    branch_own = resid_grad.astype(BF16)
    branch_own, normed_two = lax.optimization_barrier((branch_own, normed_two))
    branch = gather_start(branch_own, ranks)
    right_terms = terms_of(normed_two, gate_up_grad[:, f_part:])
    down_out = sum((part.astype(F32) for part in down_sent), down_out.astype(F32))
    mixed_own = (resid + down_out).astype(BF16)

    def heads_of(rows):
        return dot(wo_own, rows, 0, 1).astype(BF16)

    attended_grad = [heads_of(rows) for rows in branch]
    branch, right_terms, left_out = lax.optimization_barrier((branch, right_terms, left_out))
    right_out = scatter(right_terms)
    branch = gather_finish(branch, ranks)
    if ranks == 4:
        attended_grad.append(heads_of(joined(branch[-1])))
    attended_grad = jnp.stack(attended_grad)
    down_all = gather_start(down_grad, ranks)
    left_all = gather_start(left_out, ranks)
    d_heads, head_gain_parts = attend_back(
        qkv_raw, low, place, start_row, cosine, sine, head_gains, query, key, value, lse_table,
        attended, attended_grad, ranks, local, block,
    )
    d_heads, down_all, left_all, back_mixed = lax.optimization_barrier(
        (d_heads, down_all, left_all, exchange(mixed_own))
    )

    normed_grad, _, head_terms, _ = scatter_chunks(
        lambda k, given: dot(given[k], qkv_own, 0, 1).astype(BF16),
        d_heads,
        ranks,
        late=(
            (d_heads, attended),
            lambda a: head_outer(a[0], normed, a[1], branch),
        ),
    )
    head_terms, right_out = lax.optimization_barrier((head_terms, right_out))
    head_grad = scatter(head_terms)
    tok_part, attn_gain_part = rms_back(tok_f32, scale_one, attn_full, normed_grad)
    input_grad_own = (resid_grad + tok_part).astype(BF16)
    packed = jnp.concatenate(
        [
            attn_gain_part.reshape(groups, -1),
            ffn_gain_part.reshape(groups, -1),
            jnp.broadcast_to(head_gain_parts[0, :, 0], (groups, HEAD_SIZE)),
            jnp.broadcast_to(head_gain_parts[1, :, 0], (groups, HEAD_SIZE)),
        ],
        axis=1,
    )
    input_grad_own, packed, back_mixed, down_all = lax.optimization_barrier(
        (input_grad_own, packed, back_mixed, down_all)
    )
    back_grad = exchange(input_grad_own)

    down_all = gather_finish(down_all, ranks)
    left_all = gather_finish(left_all, ranks)
    right_all = gather_chunks(right_out, ranks)
    head_all = gather_chunks(head_grad, ranks)

    def of_heads(start, width):
        return widen([head_all], place, [(0, width)], width, start // width, ranks, shard)

    def of_tiles(side):
        spans = [
            (at + side * tile, at + (side + 1) * tile) for at in range(0, f_part, 2 * tile)
        ]
        return widen([left_all, right_all], place, spans, f_part, 0, ranks, shard)

    back_grad, packed, mixed, gate_out, up_out, down_out = lax.optimization_barrier(
        (
            back_grad,
            packed,
            back_mixed[send_spot],
            of_tiles(0),
            of_tiles(1),
            widen([down_all], place, [(0, f_part)], f_part, 0, ranks, shard),
        )
    )

    summed = jnp.sum(exchange(packed), axis=0)
    summed = summed.reshape(8, -1)
    for bit in range(ranks.bit_length() - 1):
        summed = summed + hop(summed, 1 << bit, ranks)
    summed = summed.reshape(-1)

    return (
        mixed,
        back_grad[send_spot],
        of_heads(0, q_part),
        of_heads(q_part, k_part),
        of_heads(q_part + k_part, k_part),
        widen([head_all], place, [(h_part, h_part + q_part)], h_part + q_part, 0, ranks, shard),
        gate_out,
        up_out,
        down_out,
        summed[:gain_rows],
        summed[gain_rows : 2 * gain_rows],
        summed[2 * gain_rows : 2 * gain_rows + HEAD_SIZE],
        summed[2 * gain_rows + HEAD_SIZE :],
    )


def solution(mesh):
    rows = P("fsdp", None)
    tokens = P(("fsdp", "seq"), None)
    in_specs = (
        tokens, tokens, rows, P(("fsdp", "seq")), rows, rows, rows, rows, rows, rows, rows,
        P("fsdp"), P("fsdp"), P(), P(),
    )
    out_specs = (
        tokens, tokens, rows, rows, rows, rows, rows, rows, rows,
        P("fsdp"), P("fsdp"), P(), P(),
    )
    return jax.shard_map(body, mesh=mesh, in_specs=in_specs, out_specs=out_specs, check_vma=False)
```
